32 devices in a mesh: prow: 8 (over y, x, core), pcol: 4 (over z).
Axes of the slice: x: 2, y: 2, z: 4, core: 2. Of those that a mesh axis runs over, the one named last changes fastest.
Arguments:
- matrix: float32 [4096, 4096], P('prow', 'pcol'), may hold values from -6 to 6
- pivots: int32 [2, 512], replicated, may hold values from 0 to 4095, as said below
- lower_inv: float32 [2, 512, 512], replicated, as said below
- upper_inv: float32 [2, 512, 512], replicated, as said below
Outputs:
- factored: float32 [4096, 4096], P('prow', 'pcol')
The draws below stay inside these ranges and needn't reach their ends.
Inputs may be any that keep to these rules, and one draw needn't show every extreme that they name: The entries of pivots[k] are distinct row indices from k * 512 to 4095. Each lower_inv[k] is lower triangular. Each upper_inv[k] is upper triangular.
All inputs are finite; a program needn't handle non-finite values.
Results may differ from the reference program's by a relative error of at most 0.0001.
Values sent between devices are 32-bit elements; how exact they have to be, the bound alone decides.
No kernel may reach another device: no remote copies, remote signals or barrier semaphores. Data moves between devices by JAX's collectives and lax.ppermute only.
A program may use at most 128 MiB of HBM per device.

```python
import jax
import jax.numpy as jnp
from jax import lax

NB = 512
PANELS = 2
N = 4096


def draw_pivots(key, part):
    panels_out = []
    for panel_index in range(PANELS):
        start_row = panel_index * NB
        end_row = start_row + NB
        panel_key = jax.random.fold_in(key, 100 + panel_index)
        window = (start_row + jax.random.permutation(jax.random.fold_in(panel_key, 1), NB)).astype(jnp.int32)
        if panel_index == 0:
            spot = jnp.argmax(window == 0)
            first_val = window[0]
            window = window.at[spot].set(first_val).at[0].set(0)
        beyond = jax.random.permutation(jax.random.fold_in(panel_key, 2), N - end_row).astype(jnp.int32)
        if panel_index == PANELS - 1:
            spot = jnp.argmax(beyond == N - end_row - 1)
            last_val = beyond[NB - 1]
            beyond = beyond.at[spot].set(last_val).at[NB - 1].set(N - end_row - 1)
        far_pool = end_row + beyond[:NB]
        kind_draw = jax.random.randint(jax.random.fold_in(panel_key, 3), (NB,), 0, 4)
        if panel_index == 0:
            kind_draw = kind_draw.at[0].set(0)
        if panel_index == PANELS - 1:
            kind_draw = kind_draw.at[NB - 1].set(3)
        panels_out.append(jnp.where(kind_draw == 3, far_pool, window))
    return jnp.stack(panels_out).astype(jnp.int32)


def triangle_factor(key, salt, lower_side):
    key_diag = jax.random.fold_in(key, salt)
    key_off = jax.random.fold_in(key, salt + 1)
    scale_all = NB ** (-0.25)
    diag_vals = jnp.exp(jax.random.uniform(key_diag, (PANELS, NB), jnp.float32, jnp.log(0.5), jnp.log(1.5)))
    off_vals = jax.random.normal(key_off, (PANELS, NB, NB), jnp.float32) * (0.5 / NB ** 0.5)
    row_idx = jnp.arange(NB)[:, None]
    col_idx = jnp.arange(NB)[None, :]
    if lower_side:
        strict = row_idx > col_idx
    else:
        strict = row_idx < col_idx
    result = jnp.where(strict[None], off_vals, 0.0) + jnp.where((row_idx == col_idx)[None], diag_vals[:, :, None], 0.0)
    return (result * scale_all).astype(jnp.float32)


def draw_lower_inv(key, part):
    return triangle_factor(key, 21, True)


def draw_upper_inv(key, part):
    return triangle_factor(key, 31, False)


def level_of(key, extent, split, smallest, high):
    def one(position, parts):
        heights = jax.random.uniform(jax.random.fold_in(jax.random.fold_in(key, 6), position), (parts,), jnp.float32, smallest / len(split), high / len(split))
        return jnp.repeat(jnp.exp(heights), extent[position] // parts).reshape((-1,) + (1,) * (len(extent) - position - 1))

    loudness = one(*split[0])
    for cut in split[1:]:
        loudness = loudness * one(*cut)
    return loudness


def centred(key, dims, scale, reach, shards=(), kind=jnp.bfloat16):
    drawn = jax.random.normal(key, dims, jnp.float32) * scale
    if len(shards) > 0:
        drawn = level_of(key, dims, shards, -0.22, 0.18) * drawn
    return jnp.clip(drawn, min=-reach, max=reach).astype(kind)


def setup_inputs(seed: int = 0) -> dict:
    key_list = jax.random.split(jax.random.key(seed), 5)
    matrix = centred(key_list[0], (N, N), 1.0, 6.0, ((0, 8), (1, 4)), jnp.float32)
    pivots = draw_pivots(jax.random.fold_in(key_list[4], 71), 0)
    lower_inv = draw_lower_inv(jax.random.fold_in(key_list[4], 71), 0)
    upper_inv = draw_upper_inv(jax.random.fold_in(key_list[4], 71), 0)
    return dict(matrix=matrix, pivots=pivots, lower_inv=lower_inv, upper_inv=upper_inv)


def compose(pivot_row, start_row, row_count):
    width = pivot_row.shape[0]
    end_row = start_row + width
    window = (start_row + jnp.arange(width, dtype=jnp.int32)).astype(jnp.int32)
    chosen = jnp.any(pivot_row[None, :] == window[:, None], axis=1)
    unnamed = jnp.logical_not(chosen)
    free_rank = (jnp.cumsum(unnamed.astype(jnp.int32)) - 1).astype(jnp.int32)
    outside = pivot_row >= end_row
    out_rank = jnp.sum((outside[None, :] & (pivot_row[None, :] < pivot_row[:, None])).astype(jnp.int32), axis=1).astype(jnp.int32)
    matches = unnamed[None, :] & (free_rank[None, :] == out_rank[:, None])
    source = jnp.sum(jnp.where(matches, window[None, :], 0), axis=1).astype(jnp.int32)
    arrangement = jnp.arange(row_count, dtype=jnp.int32).at[window].set(pivot_row.astype(jnp.int32))
    target = jnp.where(outside, pivot_row, row_count).astype(jnp.int32)
    return arrangement.at[target].set(source, mode="drop")


def product(left, right):
    return jnp.dot(left, right, precision=lax.Precision.HIGHEST, preferred_element_type=jnp.float32)


def reference(matrix, pivots, lower_inv, upper_inv):
    current = matrix
    for panel_index in range(PANELS):
        start_row = panel_index * NB
        end_row = start_row + NB
        arrangement = compose(pivots[panel_index], start_row, N)
        swapped = jnp.take(current, arrangement, axis=0)
        row_panel = product(lower_inv[panel_index], swapped[start_row:end_row, end_row:])
        column_panel = product(swapped[end_row:, start_row:end_row], upper_inv[panel_index])
        trailing = swapped[end_row:, end_row:] - product(column_panel, row_panel)
        current = swapped.at[start_row:end_row, end_row:].set(row_panel)
        current = current.at[end_row:, start_row:end_row].set(column_panel)
        current = current.at[end_row:, end_row:].set(trailing)
    return current
```

```python
import functools

import jax
import jax.numpy as jnp
from jax import lax
from jax.experimental import pallas as pl
from jax.experimental.pallas import tpu as pltpu
from jax.sharding import PartitionSpec as P

BATCH = 320
SHARE = 80


def product(left, right):
    return jnp.dot(left, right, precision=lax.Precision.HIGHEST, preferred_element_type=jnp.float32)


def displaced(pivot_row, start_row):
    width = pivot_row.shape[0]
    end_row = start_row + width
    window = start_row + jnp.arange(width, dtype=jnp.int32)
    chosen = jnp.any(pivot_row[None, :] == window[:, None], axis=1)
    unnamed = jnp.logical_not(chosen)
    free_rank = jnp.cumsum(unnamed.astype(jnp.int32)) - 1
    outside = pivot_row >= end_row
    out_rank = jnp.sum(
        (outside[None, :] & (pivot_row[None, :] < pivot_row[:, None])).astype(jnp.int32), axis=1
    )
    matches = unnamed[None, :] & (free_rank[None, :] == out_rank[:, None])
    source = jnp.sum(jnp.where(matches, window[None, :], 0), axis=1)
    return (source, outside)


def pick_body(parts, index_refs, own_ref, mate_ref, base_ref, *out_refs):
    rows = own_ref.shape[0]
    for out_ref, columns in zip(out_refs, parts):
        for list_number, first, source, target, width in columns:
            index_ref = index_refs[list_number]

            def step(i, carry):
                wanted = index_ref[first + i]
                mine, theirs = wanted - base_ref[0], wanted - base_ref[1]
                left = own_ref[pl.ds(jnp.clip(mine, 0, rows - 1), 1), source : source + width]
                right = mate_ref[pl.ds(jnp.clip(theirs, 0, rows - 1), 1), source : source + width]
                value = jnp.where((theirs >= 0) & (theirs < rows), right, 0.0)
                value = jnp.where((mine >= 0) & (mine < rows), left, value)
                out_ref[pl.ds(i, 1), target : target + width] = value
                return carry

            lax.fori_loop(0, out_ref.shape[0], step, 0, unroll=8)


def pick(own, mate, base, lists, pieces):
    half = lists[0].shape[0] // 2
    parts = []
    for side in range(2):
        target, columns = 0, []
        for number, source, width in pieces:
            columns.append((number, side * half, source, target, width))
            target += width
        parts.append(columns)
    count = len(lists)

    def body(*refs):
        pick_body(parts, refs[:count], refs[count], refs[count + 1], refs[count + 2], *refs[count + 3 :])

    smem, vmem = pl.BlockSpec(memory_space=pltpu.SMEM), pl.BlockSpec(memory_space=pltpu.VMEM)
    shape = jax.ShapeDtypeStruct((half, target), jnp.float32)
    return pl.pallas_call(
        body,
        out_shape=(shape, shape),
        in_specs=[smem] * count + [vmem, vmem, smem],
        out_specs=(vmem, vmem),
        compiler_params=pltpu.CompilerParams(vmem_limit_bytes=40 << 20),
        name="pick",
    )(*lists, own, mate, base)


def place(target, rows, where_to, count):
    def body(where_ref, count_ref, target_ref, rows_ref, out_ref):
        out_ref[...] = target_ref[...]

        def step(i, carry):
            out_ref[pl.ds(where_ref[i], 1), :] = rows_ref[pl.ds(i, 1), :]
            return carry

        lax.fori_loop(0, count_ref[0], step, 0)

    smem, vmem = pl.BlockSpec(memory_space=pltpu.SMEM), pl.BlockSpec(memory_space=pltpu.VMEM)
    return pl.pallas_call(
        body,
        out_shape=jax.ShapeDtypeStruct(target.shape, target.dtype),
        in_specs=[smem, smem, vmem, vmem],
        out_specs=vmem,
        compiler_params=pltpu.CompilerParams(vmem_limit_bytes=40 << 20),
        name="place",
    )(where_to, count, target, rows)


def flip(x, bit):
    return lax.ppermute(x, "prow", [(i, i ^ bit) for i in range(lax.axis_size("prow"))])


def gather_sum(upper, lower):
    bits, bit = [], 2
    while bit < lax.axis_size("prow"):
        bits.append(bit)
        bit *= 2
    half = len(bits) // 2
    for first, second in zip(bits, bits[half:] + bits[:half]):
        from_first, from_second = flip(upper, first), flip(lower, second)
        upper, lower = upper + from_first, lower + from_second
    mine = jnp.concatenate([upper, lower], axis=0)
    return jnp.concatenate([mine, flip(mine, 1)], axis=0)


def relay(x):
    count = lax.axis_size("pcol")
    total, current = None, x
    for even in range(2, count, 2):
        current = lax.ppermute(current, "pcol", [(even - 2, even)])
        received = current + lax.ppermute(current, "pcol", [(even, even - 1)])
        if even + 2 >= count and even + 1 < count:
            received = received + lax.ppermute(current, "pcol", [(even, even + 1)])
        total = received if total is None else total + received
    return jnp.where(lax.axis_index("pcol") == 0, x, total)


def shards(matrix, pivots, lower_inv, upper_inv):
    rows, cols = matrix.shape
    width = lower_inv.shape[1]
    devices = lax.axis_size("prow")
    if rows != width or cols < 2 * width or pivots.shape[0] != 2 or devices < 4:
        raise ValueError("unsupported shapes")
    me, column = lax.axis_index("prow"), lax.axis_index("pcol")
    core = me % 2
    first_column = column == 0
    col_ids = column * cols + jnp.arange(cols, dtype=jnp.int32)
    after_one, after_two = (col_ids >= width)[None, :], (col_ids >= 2 * width)[None, :]
    half = width // 2

    column_one = product(matrix[:, :width], upper_inv[0])
    column_one = jnp.concatenate([relay(column_one[:half]), relay(column_one[half:])], axis=0)

    named, taken = pivots[0], pivots[1]
    source_one, outside_one = displaced(named, 0)
    source_two, outside_two = displaced(taken, width)
    same = taken[:, None] == named[None, :]
    again = source_two[:, None] == named[None, :]

    def origin(hit, position):
        return jnp.where(
            jnp.any(hit, axis=1), jnp.sum(jnp.where(hit, source_one[None, :], 0), axis=1), position
        )

    second_rows = origin(same, taken)
    valid = jnp.concatenate(
        [(named >= 2 * width) & jnp.logical_not(jnp.any(same, axis=0)), outside_two]
    )
    target = jnp.concatenate([named, taken])
    origin_row = jnp.concatenate([source_one, origin(again, source_two)])
    rank = jnp.cumsum(valid.astype(jnp.int32)) - 1
    moved = jnp.sum(valid.astype(jnp.int32))
    shares = jnp.sum(
        (valid[None, :] & ((target // rows)[None, :] == jnp.arange(devices, dtype=jnp.int32)[:, None])).astype(
            jnp.int32
        ),
        axis=1,
    )

    def ours(vector):
        size = vector.shape[0] // 2
        return jnp.where(core == 0, vector[:size], vector[size:])

    def batch(start, size):
        slots = start + jnp.arange(size, dtype=jnp.int32)
        chosen = valid[None, :] & (rank[None, :] == slots[:, None])
        origins = jnp.sum(jnp.where(chosen, origin_row[None, :], 0), axis=1)
        own = valid & (rank >= start) & (rank < start + size) & (target // rows == me)
        own_rank = jnp.cumsum(own.astype(jnp.int32)) - 1
        chosen = own[None, :] & (own_rank[None, :] == jnp.arange(SHARE, dtype=jnp.int32)[:, None])
        slot = (rank - start + core * (size // 2)) % size
        own_slot = jnp.sum(jnp.where(chosen, slot[None, :], 0), axis=1)
        own_row = jnp.sum(jnp.where(chosen, (target - me * rows)[None, :], 0), axis=1)
        count = jnp.minimum(jnp.sum(own.astype(jnp.int32)), SHARE)
        return origins, own_slot, own_row, count[None]

    mate = flip(matrix, 1)
    base = jnp.stack([me * rows, (me + 1 - 2 * core) * rows]).astype(jnp.int32)

    def fetch(lists, pieces):
        return gather_sum(*pick(matrix, mate, base, [ours(v) for v in lists], pieces))

    def swap_columns(square):
        return jnp.where(core == 0, square, jnp.concatenate([square[:, half:], square[:, :half]], axis=1))

    lower_one, lower_two = swap_columns(lower_inv[0]), swap_columns(lower_inv[1])
    middle = fetch([named], [(0, width, width)])
    row_middle = product(lower_one, middle)
    column_two = product(matrix[:, width : 2 * width] - product(column_one, row_middle), upper_inv[1])
    column_two = jnp.concatenate([relay(column_two[:half]), relay(column_two[half:])], axis=0)

    origins, own_slot, own_row, count = batch(0, BATCH)
    arrived = fetch([origins], [(0, 0, cols)])

    rest = [(0, 0, width)] + ([(0, 2 * width, cols - 2 * width)] if cols > 2 * width else [])
    both = fetch([named, second_rows], rest + [(1, 0, cols)])
    first_raw = jnp.concatenate([both[:, :width], middle, both[:, width : cols - width]], axis=1)
    second_raw = both[:, cols - width :]
    row_one = product(lower_one, jnp.concatenate([both[:, :width], both[:, width : cols - width]], axis=1))
    row_one = jnp.concatenate([row_one[:, :width], row_middle, row_one[:, width:]], axis=1)
    row_one_kept = jnp.where(after_one, row_one, 0.0)

    quarter = width // 4
    top = gather_sum(*pick(column_one, flip(column_one, 1), base, [ours(second_rows)], [(0, 0, width)]))
    second_top = second_raw - product(top, row_one_kept)
    row_two = product(lower_two, second_top)
    row_two_kept = jnp.where(after_two, row_two, 0.0)

    def finish(block, one, two):
        updated = block - product(one, row_one_kept) - product(two, row_two_kept)
        left = jnp.where(first_column, one, updated[:, :width])
        middle_part = jnp.where(first_column, two, updated[:, width : 2 * width])
        return jnp.concatenate([left, middle_part, updated[:, 2 * width :]], axis=1)

    def deliver(arrived, own_slot, own_row, count, result):
        raw = jnp.take(arrived, own_slot, axis=0)
        one = product(raw[:, :width], upper_inv[0])
        two = product(raw[:, width : 2 * width] - product(one, row_middle), upper_inv[1])
        pair = relay(jnp.concatenate([one, two], axis=1))
        return place(result, finish(raw, pair[:, :width], pair[:, width:]), own_row, count)

    result = finish(matrix, column_one, column_two)
    result = deliver(arrived, own_slot, own_row, count, result)

    crowded = (moved > BATCH) | (jnp.max(shares) > SHARE)
    trips = jnp.where(crowded, (moved + SHARE - 1) // SHARE, 0)

    def more(number, result):
        origins, own_slot, own_row, count = batch(number * SHARE, SHARE)
        return deliver(fetch([origins], [(0, 0, cols)]), own_slot, own_row, count, result)

    result = lax.fori_loop(0, trips, more, result)

    left = jnp.where(first_column, top, second_top[:, :width])
    second_out = jnp.concatenate([left, second_top[:, width:]], axis=1)
    second_out = jnp.where(after_two, row_two, jnp.concatenate([second_out[half:], second_out[:half]], axis=0))
    first_out = jnp.where(after_one, row_one, first_raw)
    return jnp.where(me == 0, first_out, jnp.where(me == 1, second_out, result))


def solution(mesh):
    in_specs = (P("prow", "pcol"), P(), P(), P())
    out_specs = P("prow", "pcol")
    return jax.shard_map(shards, mesh=mesh, in_specs=in_specs, out_specs=out_specs, check_vma=False)
```

```python
import jax
import jax.numpy as jnp
from jax import lax
from jax.experimental import pallas as pl
from jax.experimental.pallas import tpu as pltpu
from jax.sharding import PartitionSpec as P

BATCH = 320
SHARE = 80
F32, BF16 = jnp.float32, jnp.bfloat16
SMEM, VMEM, ANY = (pl.BlockSpec(memory_space=space) for space in (pltpu.SMEM, pltpu.VMEM, pl.ANY))
PARAMS = pltpu.CompilerParams(vmem_limit_bytes=56 << 20)


def split(x):
    high = x.astype(BF16)
    return high, (x - high.astype(F32)).astype(BF16)


def mul(left, right):
    dot = lambda a, b: jnp.dot(a, b, preferred_element_type=F32)
    return dot(left[0], right[0]) + (dot(left[0], right[1]) + dot(left[1], right[0]))


def product(left, right):
    return jnp.dot(left, right, precision=lax.Precision.HIGH, preferred_element_type=F32)


def displaced(pivot_row, start_row):
    width = pivot_row.shape[0]
    end_row = start_row + width
    window = start_row + jnp.arange(width, dtype=jnp.int32)
    chosen = jnp.any(pivot_row[None, :] == window[:, None], axis=1)
    unnamed = jnp.logical_not(chosen)
    free_rank = jnp.cumsum(unnamed.astype(jnp.int32)) - 1
    outside = pivot_row >= end_row
    out_rank = jnp.sum(
        (outside[None, :] & (pivot_row[None, :] < pivot_row[:, None])).astype(jnp.int32), axis=1
    )
    matches = unnamed[None, :] & (free_rank[None, :] == out_rank[:, None])
    source = jnp.sum(jnp.where(matches, window[None, :], 0), axis=1)
    return (source, outside)


def pick(own, mate, lists, pieces, shape):
    rows, cols = own.shape
    count = len(lists)

    def body(*refs):
        index_refs, (own_ref, mate_ref, out_ref, chip, sems) = refs[:count], refs[count:]
        copies = [
            pltpu.make_async_copy(own_ref, chip.at[pl.ds(0, rows)], sems.at[0]),
            pltpu.make_async_copy(mate_ref, chip.at[pl.ds(rows, rows)], sems.at[1]),
        ]
        for copy in copies:
            copy.start()
        for copy in copies:
            copy.wait()
        for number, source, row, column, width in pieces:

            def step(i, carry):
                wanted = index_refs[number][i]
                value = chip[pl.ds(jnp.maximum(wanted, 0), 1), source : source + width]
                out_ref[pl.ds(row + i, 1), column : column + width] = jnp.where(wanted >= 0, value, 0.0)
                return carry

            lax.fori_loop(0, lists[number].shape[0], step, 0, unroll=8)

    return pl.pallas_call(
        body,
        out_shape=jax.ShapeDtypeStruct(shape, F32),
        in_specs=[SMEM] * count + [ANY, ANY],
        out_specs=VMEM,
        scratch_shapes=[pltpu.VMEM((2 * rows, cols), F32), pltpu.SemaphoreType.DMA((2,))],
        compiler_params=PARAMS,
        name="pick",
    )(*lists, own, mate)


def middle_step(matrix, one, mine, mate, lower, upper_one, upper_two, core, slots, targets, count, size):
    rows, cols = matrix.shape
    width = lower.shape[0]
    half = width // 2
    blocks = cols // width
    part = (rows + SHARE) // 2

    def body(core_ref, slot_ref, target_ref, count_ref, matrix_ref, one_ref, mine_ref, mate_ref, lower_ref, u1_ref, u2_ref,
             block_ref, upper_ref, under_ref, panel_ref, raw, pair, new_one):
        block_ref[...] = matrix_ref[...]
        raw[...] = jnp.zeros_like(raw)

        def bring(i, carry):
            slot, row = slot_ref[i], target_ref[i]
            here = slot < size
            at = half + jnp.where(here, slot, slot - size)
            for b in range(blocks):
                value = jnp.where(here, mine_ref[pl.ds(at + b * size, 1), :], mate_ref[pl.ds(at + b * size, 1), :])
                block_ref[pl.ds(row, 1), b * width : (b + 1) * width] = value
                if b == 0:
                    raw[pl.ds(i, 1), :] = value
            return carry

        lax.fori_loop(0, count_ref[0], bring, 0)
        fresh = mul(split(raw[...]), split(u1_ref[...]))
        pair[pl.ds(rows, SHARE), :] = fresh
        new_one[...] = one_ref[...]

        def renew(i, carry):
            new_one[pl.ds(target_ref[i], 1), :] = pair[pl.ds(rows + i, 1), :]
            return carry

        lax.fori_loop(0, count_ref[0], renew, 0)
        first = pl.multiple_of(core_ref[0] * half, half)
        second = pl.multiple_of(half - core_ref[0] * half, half)
        panel = mul(split(lower_ref[:, pl.ds(first, half)]), split(mine_ref[:half, :])) + mul(
            split(lower_ref[:, pl.ds(second, half)]), split(mate_ref[:half, :])
        )
        panel_ref[...] = panel
        rest = block_ref[:, width : 2 * width] - mul(split(new_one[...]), split(panel))
        pair[pl.ds(0, rows), :] = mul(split(rest), split(u2_ref[...]))
        upper_ref[...] = pair[:part, :]
        under_ref[...] = pair[part:, :]

    shape = lambda *s: jax.ShapeDtypeStruct(s, F32)
    return pl.pallas_call(
        body,
        out_shape=(shape(rows, cols), shape(part, width), shape(part, width), shape(width, width)),
        in_specs=[SMEM] * 4 + [VMEM] * 7,
        out_specs=(VMEM,) * 4,
        scratch_shapes=[pltpu.VMEM(s, F32) for s in ((SHARE, width), (rows + SHARE, width), (rows, width))],
        compiler_params=PARAMS,
        name="middle",
    )(core, slots, targets, count, matrix, one, mine, mate, lower, upper_one, upper_two)


def row_step(where, panel, mine, mate, top_mine, top_mate, lower, cols):
    width = panel.shape[0]
    half = width // 2
    blocks = cols // width
    offset = cols - width

    def body(where_ref, panel_ref, mine_ref, mate_ref, tm_ref, tt_ref, lower_ref, high_ref, low_ref, edge_ref, second):
        me, first_column = where_ref[0], where_ref[1] == 0
        core = me % 2
        first = pl.multiple_of(core * half, half)
        other = pl.multiple_of(half - core * half, half)
        lower = lambda k: (split(lower_ref[k, :, pl.ds(first, half)]), split(lower_ref[k, :, pl.ds(other, half)]))
        one, two = lower(0), lower(1)
        tops = (split(tm_ref[...]), split(tt_ref[...]))
        for b in range(blocks):
            at = slice(b * width, (b + 1) * width)
            source = slice((b if b < 1 else b - 1) * width, ((b if b < 1 else b - 1) + 1) * width)
            if b == 1:
                row_one = panel_ref[...]
            else:
                row_one = mul(one[0], split(mine_ref[:, source])) + mul(one[1], split(mate_ref[:, source]))
            kept = jnp.where(first_column, 0.0, row_one) if b < 1 else row_one
            pair = split(kept)
            high_ref[:width, at], low_ref[:width, at] = pair
            rest = slice(offset + b * width, offset + (b + 1) * width)
            second[:half, :] = mine_ref[:, rest] - mul(tops[0], pair)
            second[half:, :] = mate_ref[:, rest] - mul(tops[1], pair)
            row_two = mul(two[0], split(second[:half, :])) + mul(two[1], split(second[half:, :]))
            kept = jnp.where(first_column, 0.0, row_two) if b < 2 else row_two
            high_ref[width:, at], low_ref[width:, at] = split(kept)

            @pl.when(me == 0)
            def _():
                if b >= 1:
                    edge_ref[:, at] = row_one
                else:
                    edge_ref[:half, at] = jnp.where(first_column, mine_ref[:, source], row_one[:half, :])
                    edge_ref[half:, at] = jnp.where(first_column, mate_ref[:, source], row_one[half:, :])

            @pl.when(me != 0)
            def _():
                if b >= 2:
                    edge_ref[:, at] = row_two
                elif b == 1:
                    edge_ref[:half, at] = jnp.where(first_column, second[half:, :], row_two[:half, :])
                    edge_ref[half:, at] = jnp.where(first_column, second[:half, :], row_two[half:, :])
                else:
                    edge_ref[:half, at] = jnp.where(first_column, tt_ref[...], row_two[:half, :])
                    edge_ref[half:, at] = jnp.where(first_column, tm_ref[...], row_two[half:, :])

    return pl.pallas_call(
        body,
        out_shape=(
            jax.ShapeDtypeStruct((2 * width, cols), BF16),
            jax.ShapeDtypeStruct((2 * width, cols), BF16),
            jax.ShapeDtypeStruct((width, cols), F32),
        ),
        in_specs=[SMEM] + [VMEM] * 6,
        out_specs=(VMEM,) * 3,
        scratch_shapes=[pltpu.VMEM((width, width), F32)],
        compiler_params=PARAMS,
        name="rows",
    )(where, panel, mine, mate, top_mine, top_mate, lower)


def finish_step(where, targets, count, block, ones, uppers, unders, high, low, edge, held):
    rows, cols = block.shape
    width = ones[0].shape[1]
    part = uppers[0].shape[0]
    parts = len(ones)
    chunk = min(rows, 128)

    def body(*refs):
        where_ref, target_ref, count_ref, block_ref, high_ref, low_ref = refs[:6]
        one_refs, upper_refs, under_refs = (refs[6 + parts * k : 6 + parts * (k + 1)] for k in range(3))
        edge_ref, out_ref, one, pair, sems = refs[6 + 3 * parts :]
        me, column = where_ref[0], where_ref[1]
        first_column = column == 0
        for k in range(parts):
            mine = column == held[k][0]
            for z in held[k][1:]:
                mine = mine | (column == z)

            @pl.when((me >= 2) & mine)
            def _():
                copies = [
                    pltpu.make_async_copy(one_refs[k], one, sems.at[0]),
                    pltpu.make_async_copy(upper_refs[k], pair.at[pl.ds(0, part)], sems.at[1]),
                    pltpu.make_async_copy(under_refs[k], pair.at[pl.ds(part, part)], sems.at[2]),
                ]
                for copy in copies:
                    copy.start()
                for copy in copies:
                    copy.wait()

        @pl.when(me < 2)
        def _():
            copy = pltpu.make_async_copy(edge_ref, out_ref, sems.at[0])
            copy.start()
            copy.wait()

        @pl.when(me >= 2)
        def _():
            def renew(i, carry):
                one[pl.ds(target_ref[i], 1), :] = pair[pl.ds(rows + i, 1), :]
                return carry

            lax.fori_loop(0, count_ref[0], renew, 0)

            @pl.loop(0, rows // chunk)
            def _(c):
                at = pl.ds(pl.multiple_of(c * chunk, chunk), chunk)
                left = jnp.concatenate([one[at, :], pair[at, :]], axis=1)
                total = block_ref[at, :] - mul(split(left), (high_ref[...], low_ref[...]))
                out_ref[at, : 2 * width] = jnp.where(first_column, left, total[:, : 2 * width])
                if cols > 2 * width:
                    out_ref[at, 2 * width :] = total[:, 2 * width :]

    return pl.pallas_call(
        body,
        out_shape=jax.ShapeDtypeStruct((rows, cols), F32),
        in_specs=[SMEM] * 3 + [VMEM] * 3 + [ANY] * (3 * parts + 1),
        out_specs=VMEM,
        scratch_shapes=[
            pltpu.VMEM((rows, width), F32),
            pltpu.VMEM((rows + SHARE, width), F32),
            pltpu.SemaphoreType.DMA((3,)),
        ],
        compiler_params=PARAMS,
        name="finish",
    )(where, targets, count, block, high, low, *ones, *uppers, *unders, edge)


def place(target, rows, where_to, count):
    def body(where_ref, count_ref, target_ref, rows_ref, out_ref):
        out_ref[...] = target_ref[...]

        def step(i, carry):
            out_ref[pl.ds(where_ref[i], 1), :] = rows_ref[pl.ds(i, 1), :]
            return carry

        lax.fori_loop(0, count_ref[0], step, 0)

    return pl.pallas_call(
        body,
        out_shape=jax.ShapeDtypeStruct(target.shape, target.dtype),
        in_specs=[SMEM, SMEM, VMEM, VMEM],
        out_specs=VMEM,
        compiler_params=PARAMS,
        name="place",
    )(where_to, count, target, rows)


def swap_cores(x):
    return lax.ppermute(x, "prow", [(i, i ^ 1) for i in range(lax.axis_size("prow"))])


def gather_sum(x):
    devices = lax.axis_size("prow")
    bits = [1 << k for k in range(1, devices.bit_length() - 1)]
    turned = bits[len(bits) // 2 :] + bits[: len(bits) // 2]
    for first, second in zip(bits, turned):
        x = x + lax.ppermute(x, "prow", [(i, i ^ (second if i % 2 else first)) for i in range(devices)])
    return x, swap_cores(x)


def relay(x):
    count = lax.axis_size("pcol")
    parts = [x]
    for even in range(2, count, 2):
        current = lax.ppermute(x if even == 2 else parts[-2 if even > 4 else 1], "pcol", [(even - 2, even)])
        parts += [current, lax.ppermute(current, "pcol", [(even, even - 1)])]
        if even + 2 >= count and even + 1 < count:
            parts.append(lax.ppermute(current, "pcol", [(even, even + 1)]))
    return parts


def held_by(count):
    held = [[0]]
    for even in range(2, count, 2):
        held += [[even], [even - 1]]
        if even + 2 >= count and even + 1 < count:
            held.append([even + 1])
    return held


def joined(parts):
    total = parts[1]
    for part in parts[2:]:
        total = total + part
    return jnp.where(lax.axis_index("pcol") == 0, parts[0], total)


def shards(matrix, pivots, lower_inv, upper_inv):
    rows, cols = matrix.shape
    width = lower_inv.shape[1]
    devices = lax.axis_size("prow")
    if rows != width or cols < 2 * width or cols % width or pivots.shape[0] != 2 or devices < 4:
        raise ValueError("unsupported shapes")
    me, column = lax.axis_index("prow"), lax.axis_index("pcol")
    core = me % 2
    first_column = column == 0
    half = width // 2
    blocks = cols // width
    mate = swap_cores(matrix)

    column_one = product(matrix[:, :width], upper_inv[0])
    ones = relay(column_one)

    named, taken = pivots[0], pivots[1]
    source_one, outside_one = displaced(named, 0)
    source_two, outside_two = displaced(taken, width)
    same = taken[:, None] == named[None, :]
    again = source_two[:, None] == named[None, :]

    def origin(hit, position):
        return jnp.where(
            jnp.any(hit, axis=1), jnp.sum(jnp.where(hit, source_one[None, :], 0), axis=1), position
        )

    second_rows = origin(same, taken)
    valid = jnp.concatenate(
        [(named >= 2 * width) & jnp.logical_not(jnp.any(same, axis=0)), outside_two]
    )
    target = jnp.concatenate([named, taken])
    origin_row = jnp.concatenate([source_one, origin(again, source_two)])
    rank = jnp.cumsum(valid.astype(jnp.int32)) - 1
    moved = jnp.sum(valid.astype(jnp.int32))
    shares = jnp.sum(
        (valid[None, :] & ((target // rows)[None, :] == jnp.arange(devices, dtype=jnp.int32)[:, None])).astype(
            jnp.int32
        ),
        axis=1,
    )

    def ours(vector):
        size = vector.shape[0] // 2
        wanted = jnp.where(core == 0, vector[:size], vector[size:])
        mine, theirs = wanted - me * rows, wanted - (me + 1 - 2 * core) * rows
        inside = lambda v: (v >= 0) & (v < rows)
        return jnp.where(inside(mine), mine, jnp.where(inside(theirs), rows + theirs, -1))

    def batch(start, size):
        slots = start + jnp.arange(size, dtype=jnp.int32)
        chosen = valid[None, :] & (rank[None, :] == slots[:, None])
        origins = jnp.sum(jnp.where(chosen, origin_row[None, :], 0), axis=1)
        own = valid & (rank >= start) & (rank < start + size) & (target // rows == me)
        own_rank = jnp.cumsum(own.astype(jnp.int32)) - 1
        chosen = own[None, :] & (own_rank[None, :] == jnp.arange(SHARE, dtype=jnp.int32)[:, None])
        slot = (rank - start + core * (size // 2)) % size
        own_slot = jnp.sum(jnp.where(chosen, slot[None, :], 0), axis=1)
        own_row = jnp.sum(jnp.where(chosen, (target - me * rows)[None, :], 0), axis=1)
        count = jnp.minimum(jnp.sum(own.astype(jnp.int32)), SHARE)
        return ours(origins), own_slot, own_row, count[None]

    origins, own_slot, own_row, count = batch(0, BATCH)
    size = BATCH // 2
    lists = [ours(named), origins]
    pieces = [(0, width, 0, 0, width)] + [(1, b * width, half + b * size, 0, width) for b in range(blocks)]
    mine, mates = gather_sum(pick(matrix, mate, lists, pieces, (half + blocks * size, width)))
    block, upper, under, panel = middle_step(
        matrix, column_one, mine, mates, lower_inv[0], upper_inv[0], upper_inv[1], core[None], own_slot, own_row, count, size
    )
    uppers, unders = relay(upper), relay(under)

    lists = [ours(named), ours(second_rows)]
    pieces = [(0, 0, 0, 0, width)] + [(0, b * width, 0, (b - 1) * width, width) for b in range(2, blocks)]
    pieces += [(1, 0, 0, cols - width, cols)]
    mine, mates = gather_sum(pick(matrix, mate, lists, pieces, (half, 2 * cols - width)))

    one = joined(ones)
    top_mine, top_mate = gather_sum(pick(one, swap_cores(one), [ours(second_rows)], [(0, 0, 0, 0, width)], (half, width)))
    where = jnp.stack([me, column]).astype(jnp.int32)
    high, low, edge = row_step(where, panel, mine, mates, top_mine, top_mate, lower_inv, cols)
    held = held_by(lax.axis_size("pcol"))
    result = finish_step(where, own_row, count, block, ones, uppers, unders, high, low, edge, held)

    crowded = (moved > BATCH) | (jnp.max(shares) > SHARE)
    trips = jnp.where(crowded, (moved + SHARE - 1) // SHARE, 0)

    def more(number, result):
        origins, own_slot, own_row, count = batch(number * SHARE, SHARE)
        rows_here = gather_sum(pick(matrix, mate, [origins], [(0, 0, 0, 0, cols)], (SHARE // 2, cols)))
        raw = jnp.take(jnp.concatenate(rows_here, axis=0), own_slot, axis=0)
        one = product(raw[:, :width], upper_inv[0])
        two = product(raw[:, width : 2 * width] - product(one, panel), upper_inv[1])
        pair = joined(relay(jnp.concatenate([one, two], axis=1)))
        panels = high.astype(F32) + low.astype(F32)
        updated = raw - product(pair, panels)
        updated = jnp.concatenate(
            [jnp.where(first_column, pair, updated[:, : 2 * width]), updated[:, 2 * width :]], axis=1
        )
        return place(result, updated, own_row, count)

    return lax.fori_loop(0, trips, more, result)


def solution(mesh):
    in_specs = (P("prow", "pcol"), P(), P(), P())
    out_specs = P("prow", "pcol")
    return jax.shard_map(shards, mesh=mesh, in_specs=in_specs, out_specs=out_specs, check_vma=False)
```

```python
import jax
import jax.numpy as jnp
from jax import lax
from jax.experimental import pallas as pl
from jax.experimental.pallas import tpu as pltpu
from jax.sharding import PartitionSpec as P

BATCH = 320
SHARE = 80
F32, BF16 = jnp.float32, jnp.bfloat16
SMEM, VMEM, ANY = (pl.BlockSpec(memory_space=space) for space in (pltpu.SMEM, pltpu.VMEM, pl.ANY))
COSTS = dict(middle=6000000000, rows=10000000000, finish=10000000000, place=1)
PARAMS = pltpu.CompilerParams(vmem_limit_bytes=56 << 20)


def cost(work):
    return pl.CostEstimate(flops=work, bytes_accessed=1, transcendentals=0)


def split(x):
    high = x.astype(BF16)
    return high, (x - high.astype(F32)).astype(BF16)


def mul(left, right):
    dot = lambda a, b: jnp.dot(a, b, preferred_element_type=F32)
    return dot(left[0], right[0]) + (dot(left[0], right[1]) + dot(left[1], right[0]))


def product(left, right):
    return jnp.dot(left, right, precision=lax.Precision.HIGH, preferred_element_type=F32)


def displaced(pivot_row, start_row):
    width = pivot_row.shape[0]
    end_row = start_row + width
    window = start_row + jnp.arange(width, dtype=jnp.int32)
    chosen = jnp.any(pivot_row[None, :] == window[:, None], axis=1)
    unnamed = jnp.logical_not(chosen)
    free_rank = jnp.cumsum(unnamed.astype(jnp.int32)) - 1
    outside = pivot_row >= end_row
    out_rank = jnp.sum(
        (outside[None, :] & (pivot_row[None, :] < pivot_row[:, None])).astype(jnp.int32), axis=1
    )
    matches = unnamed[None, :] & (free_rank[None, :] == out_rank[:, None])
    source = jnp.sum(jnp.where(matches, window[None, :], 0), axis=1)
    return (source, outside)


def pick(sources, lists, pieces, shapes, choice=None, work=1):
    rows, cols = sources[0].shape
    count, many = len(lists), len(sources)
    stacked = 1 if choice else many

    def body(*refs):
        index_refs, source_refs, rest = refs[:count], refs[count : count + many], refs[count + many :]
        if choice:
            where_ref, rest = rest[0], rest[1:]
        out_refs, (chip, sems) = rest[: len(shapes)], rest[len(shapes) :]
        if choice:
            for ref, places in zip(source_refs, choice[1]):

                @pl.when(among(where_ref[1], places))
                def _():
                    copy = pltpu.make_async_copy(ref, chip, sems.at[0])
                    copy.start()
                    copy.wait()
        else:
            copies = [
                pltpu.make_async_copy(ref, chip.at[pl.ds(k * rows, rows)], sems.at[k])
                for k, ref in enumerate(source_refs)
            ]
            for copy in copies:
                copy.start()
            for copy in copies:
                copy.wait()
        for index_ref, vector, segments in zip(index_refs, lists, pieces):

            def step(i, carry):
                wanted = index_ref[i]
                at = pl.ds(jnp.maximum(wanted, 0), 1)
                for output, source, row, column, width in segments:
                    value = jnp.where(wanted >= 0, chip[at, source : source + width], 0.0)
                    out_refs[output][pl.ds(row + i, 1), column : column + width] = value
                return carry

            lax.fori_loop(0, vector.shape[0], step, 0, unroll=8)

    return pl.pallas_call(
        body,
        out_shape=[jax.ShapeDtypeStruct(shape, F32) for shape in shapes],
        in_specs=[SMEM] * count + [ANY] * many + ([SMEM] if choice else []),
        out_specs=[VMEM] * len(shapes),
        scratch_shapes=[pltpu.VMEM((stacked * rows, cols), F32), pltpu.SemaphoreType.DMA((stacked,))],
        compiler_params=PARAMS,
        cost_estimate=cost(work),
        name="pick",
    )(*lists, *sources, *([choice[0]] if choice else []))


def among(value, places):
    found = value == places[0]
    for place in places[1:]:
        found = found | (value == place)
    return found


def middle_step(matrix, one, mine, mate, lower, upper, core, slots, targets, count, size):
    rows, cols = matrix.shape
    width = lower.shape[1]
    half = width // 2
    blocks = cols // width
    part = (rows + SHARE) // 2

    def body(core_ref, slot_ref, target_ref, count_ref, matrix_ref, one_ref, mine_ref, mate_ref, lower_ref, u_ref,
             block_ref, upper_ref, under_ref, panel_ref, raw, pair, new_one):
        block_ref[...] = matrix_ref[...]
        raw[...] = jnp.zeros_like(raw)

        def bring(i, carry):
            slot, row = slot_ref[i], target_ref[i]
            here = slot < size
            at = half + jnp.where(here, slot, slot - size)
            for b in range(blocks):
                value = jnp.where(here, mine_ref[pl.ds(at + b * size, 1), :], mate_ref[pl.ds(at + b * size, 1), :])
                block_ref[pl.ds(row, 1), b * width : (b + 1) * width] = value
                if b == 0:
                    raw[pl.ds(i, 1), :] = value
            return carry

        lax.fori_loop(0, count_ref[0], bring, 0)
        fresh = mul(split(raw[...]), split(u_ref[0]))
        pair[pl.ds(rows, SHARE), :] = fresh
        new_one[...] = one_ref[...]

        def renew(i, carry):
            new_one[pl.ds(target_ref[i], 1), :] = pair[pl.ds(rows + i, 1), :]
            return carry

        lax.fori_loop(0, count_ref[0], renew, 0)
        first = pl.multiple_of(core_ref[0] * half, half)
        second = pl.multiple_of(half - core_ref[0] * half, half)
        panel = mul(split(lower_ref[0, :, pl.ds(first, half)]), split(mine_ref[:half, :])) + mul(
            split(lower_ref[0, :, pl.ds(second, half)]), split(mate_ref[:half, :])
        )
        panel_ref[...] = panel
        rest = block_ref[:, width : 2 * width] - mul(split(new_one[...]), split(panel))
        pair[pl.ds(0, rows), :] = mul(split(rest), split(u_ref[1]))
        upper_ref[...] = pair[:part, :]
        under_ref[...] = pair[part:, :]

    shape = lambda *s: jax.ShapeDtypeStruct(s, F32)
    return pl.pallas_call(
        body,
        out_shape=(shape(rows, cols), shape(part, width), shape(part, width), shape(width, width)),
        in_specs=[SMEM] * 4 + [VMEM] * 6,
        out_specs=(VMEM,) * 4,
        scratch_shapes=[pltpu.VMEM(s, F32) for s in ((SHARE, width), (rows + SHARE, width), (rows, width))],
        compiler_params=PARAMS,
        cost_estimate=cost(COSTS["middle"]),
        name="middle",
    )(core, slots, targets, count, matrix, one, mine, mate, lower, upper)


def row_step(where, panel, mine, mate, top_mine, top_mate, lower, cols):
    width = panel.shape[0]
    half = width // 2
    blocks = cols // width
    offset = cols - width

    def body(where_ref, panel_ref, mine_ref, mate_ref, tm_ref, tt_ref, lower_ref, high_ref, low_ref, edge_ref, second):
        me, first_column = where_ref[0], where_ref[1] == 0
        core = me % 2
        first = pl.multiple_of(core * half, half)
        other = pl.multiple_of(half - core * half, half)
        lower = lambda k: (split(lower_ref[k, :, pl.ds(first, half)]), split(lower_ref[k, :, pl.ds(other, half)]))
        one, two = lower(0), lower(1)
        tops = (split(tm_ref[...]), split(tt_ref[...]))
        for b in range(blocks):
            at = slice(b * width, (b + 1) * width)
            source = slice((b if b < 1 else b - 1) * width, ((b if b < 1 else b - 1) + 1) * width)
            if b == 1:
                row_one = panel_ref[...]
            else:
                row_one = mul(one[0], split(mine_ref[:, source])) + mul(one[1], split(mate_ref[:, source]))
            kept = jnp.where(first_column, 0.0, row_one) if b < 1 else row_one
            pair = split(kept)
            high_ref[:width, at], low_ref[:width, at] = pair
            rest = slice(offset + b * width, offset + (b + 1) * width)
            second[:half, :] = mine_ref[:, rest] - mul(tops[0], pair)
            second[half:, :] = mate_ref[:, rest] - mul(tops[1], pair)
            row_two = mul(two[0], split(second[:half, :])) + mul(two[1], split(second[half:, :]))
            kept = jnp.where(first_column, 0.0, row_two) if b < 2 else row_two
            high_ref[width:, at], low_ref[width:, at] = split(kept)

            @pl.when(me == 0)
            def _():
                if b >= 1:
                    edge_ref[:, at] = row_one
                else:
                    edge_ref[:half, at] = jnp.where(first_column, mine_ref[:, source], row_one[:half, :])
                    edge_ref[half:, at] = jnp.where(first_column, mate_ref[:, source], row_one[half:, :])

            @pl.when(me != 0)
            def _():
                if b >= 2:
                    edge_ref[:, at] = row_two
                elif b == 1:
                    edge_ref[:half, at] = jnp.where(first_column, second[half:, :], row_two[:half, :])
                    edge_ref[half:, at] = jnp.where(first_column, second[:half, :], row_two[half:, :])
                else:
                    edge_ref[:half, at] = jnp.where(first_column, tt_ref[...], row_two[:half, :])
                    edge_ref[half:, at] = jnp.where(first_column, tm_ref[...], row_two[half:, :])

    return pl.pallas_call(
        body,
        out_shape=(
            jax.ShapeDtypeStruct((2 * width, cols), BF16),
            jax.ShapeDtypeStruct((2 * width, cols), BF16),
            jax.ShapeDtypeStruct((width, cols), F32),
        ),
        in_specs=[SMEM] + [VMEM] * 6,
        out_specs=(VMEM,) * 3,
        scratch_shapes=[pltpu.VMEM((width, width), F32)],
        compiler_params=PARAMS,
        cost_estimate=cost(COSTS["rows"]),
        name="rows",
    )(where, panel, mine, mate, top_mine, top_mate, lower)


def finish_step(where, targets, count, block, ones, uppers, unders, high, low, edge, held):
    rows, cols = block.shape
    width = ones[0].shape[1]
    part = uppers[0].shape[0]
    parts = len(ones)
    chunk = min(rows, 128)

    def body(*refs):
        where_ref, target_ref, count_ref, block_ref, high_ref, low_ref = refs[:6]
        one_refs, upper_refs, under_refs = (refs[6 + parts * k : 6 + parts * (k + 1)] for k in range(3))
        edge_ref, out_ref, one, pair, sems = refs[6 + 3 * parts :]
        me, column = where_ref[0], where_ref[1]
        first_column = column == 0
        for k in range(parts):

            @pl.when((me >= 2) & among(column, held[k]))
            def _():
                copies = [
                    pltpu.make_async_copy(one_refs[k], one, sems.at[0]),
                    pltpu.make_async_copy(upper_refs[k], pair.at[pl.ds(0, part)], sems.at[1]),
                    pltpu.make_async_copy(under_refs[k], pair.at[pl.ds(part, part)], sems.at[2]),
                ]
                for copy in copies:
                    copy.start()
                for copy in copies:
                    copy.wait()

        @pl.when(me < 2)
        def _():
            copy = pltpu.make_async_copy(edge_ref, out_ref, sems.at[0])
            copy.start()
            copy.wait()

        @pl.when(me >= 2)
        def _():
            def renew(i, carry):
                one[pl.ds(target_ref[i], 1), :] = pair[pl.ds(rows + i, 1), :]
                return carry

            lax.fori_loop(0, count_ref[0], renew, 0)

            @pl.loop(0, rows // chunk)
            def _(c):
                at = pl.ds(pl.multiple_of(c * chunk, chunk), chunk)
                left = jnp.concatenate([one[at, :], pair[at, :]], axis=1)
                total = block_ref[at, :] - mul(split(left), (high_ref[...], low_ref[...]))
                out_ref[at, : 2 * width] = jnp.where(first_column, left, total[:, : 2 * width])
                if cols > 2 * width:
                    out_ref[at, 2 * width :] = total[:, 2 * width :]

    return pl.pallas_call(
        body,
        out_shape=jax.ShapeDtypeStruct((rows, cols), F32),
        in_specs=[SMEM] * 3 + [VMEM] * 3 + [ANY] * (3 * parts + 1),
        out_specs=VMEM,
        scratch_shapes=[
            pltpu.VMEM((rows, width), F32),
            pltpu.VMEM((rows + SHARE, width), F32),
            pltpu.SemaphoreType.DMA((3,)),
        ],
        compiler_params=PARAMS,
        cost_estimate=cost(COSTS["finish"]),
        name="finish",
    )(where, targets, count, block, high, low, *ones, *uppers, *unders, edge)


def place(target, rows, where_to, count):
    def body(where_ref, count_ref, target_ref, rows_ref, out_ref):
        out_ref[...] = target_ref[...]

        def step(i, carry):
            out_ref[pl.ds(where_ref[i], 1), :] = rows_ref[pl.ds(i, 1), :]
            return carry

        lax.fori_loop(0, count_ref[0], step, 0)

    return pl.pallas_call(
        body,
        out_shape=jax.ShapeDtypeStruct(target.shape, target.dtype),
        in_specs=[SMEM, SMEM, VMEM, VMEM],
        out_specs=VMEM,
        compiler_params=PARAMS,
        cost_estimate=cost(COSTS["place"]),
        name="place",
    )(where_to, count, target, rows)


def swap_cores(x):
    return lax.ppermute(x, "prow", [(i, i ^ 1) for i in range(lax.axis_size("prow"))])


def axes_order():
    bits = [1 << k for k in range(1, lax.axis_size("prow").bit_length() - 1)]
    return list(zip(bits, bits[len(bits) // 2 :] + bits[: len(bits) // 2]))


def flip_axes(x, pair):
    first, second = pair
    return lax.ppermute(x, "prow", [(i, i ^ (second if i % 2 else first)) for i in range(lax.axis_size("prow"))])


def gather_sum(x, steps=None):
    for pair in axes_order() if steps is None else steps:
        x = x + flip_axes(x, pair)
    return x, swap_cores(x)


def first_hop(x):
    return lax.ppermute(x, "pcol", [(0, 2)])


def onward(x, current):
    count = lax.axis_size("pcol")
    parts = [x]
    for even in range(2, count, 2):
        parts += [current, lax.ppermute(current, "pcol", [(even, even - 1)])]
        if even + 2 < count:
            current = lax.ppermute(current, "pcol", [(even, even + 2)])
        elif even + 1 < count:
            parts.append(lax.ppermute(current, "pcol", [(even, even + 1)]))
    return parts


def relay(x):
    return onward(x, first_hop(x))


def after(x, *others):
    return lax.optimization_barrier((x, *others))[0]


def held_by(count):
    held = [[0]]
    for even in range(2, count, 2):
        held += [[even], [even - 1]]
        if even + 2 >= count and even + 1 < count:
            held.append([even + 1])
    return held


def joined(parts):
    total = parts[1]
    for part in parts[2:]:
        total = total + part
    return jnp.where(lax.axis_index("pcol") == 0, parts[0], total)


def shards(matrix, pivots, lower_inv, upper_inv):
    rows, cols = matrix.shape
    width = lower_inv.shape[1]
    devices = lax.axis_size("prow")
    if rows != width or cols < 2 * width or cols % width or pivots.shape[0] != 2 or devices < 4:
        raise ValueError("unsupported shapes")
    me, column = lax.axis_index("prow"), lax.axis_index("pcol")
    core = me % 2
    first_column = column == 0
    half = width // 2
    blocks = cols // width
    mate = swap_cores(matrix)

    column_one = product(matrix[:, :width], upper_inv[0])
    hop = first_hop(column_one)

    named, taken = pivots[0], pivots[1]
    source_one, outside_one = displaced(named, 0)
    source_two, outside_two = displaced(taken, width)
    same = taken[:, None] == named[None, :]
    again = source_two[:, None] == named[None, :]

    def origin(hit, position):
        return jnp.where(
            jnp.any(hit, axis=1), jnp.sum(jnp.where(hit, source_one[None, :], 0), axis=1), position
        )

    second_rows = origin(same, taken)
    valid = jnp.concatenate(
        [(named >= 2 * width) & jnp.logical_not(jnp.any(same, axis=0)), outside_two]
    )
    target = jnp.concatenate([named, taken])
    origin_row = jnp.concatenate([source_one, origin(again, source_two)])
    rank = jnp.cumsum(valid.astype(jnp.int32)) - 1
    moved = jnp.sum(valid.astype(jnp.int32))
    shares = jnp.sum(
        (valid[None, :] & ((target // rows)[None, :] == jnp.arange(devices, dtype=jnp.int32)[:, None])).astype(
            jnp.int32
        ),
        axis=1,
    )

    def ours(vector):
        size = vector.shape[0] // 2
        wanted = jnp.where(core == 0, vector[:size], vector[size:])
        mine, theirs = wanted - me * rows, wanted - (me + 1 - 2 * core) * rows
        inside = lambda v: (v >= 0) & (v < rows)
        return jnp.where(inside(mine), mine, jnp.where(inside(theirs), rows + theirs, -1))

    def batch(start, size):
        slots = start + jnp.arange(size, dtype=jnp.int32)
        chosen = valid[None, :] & (rank[None, :] == slots[:, None])
        origins = jnp.sum(jnp.where(chosen, origin_row[None, :], 0), axis=1)
        own = valid & (rank >= start) & (rank < start + size) & (target // rows == me)
        own_rank = jnp.cumsum(own.astype(jnp.int32)) - 1
        chosen = own[None, :] & (own_rank[None, :] == jnp.arange(SHARE, dtype=jnp.int32)[:, None])
        slot = (rank - start + core * (size // 2)) % size
        own_slot = jnp.sum(jnp.where(chosen, slot[None, :], 0), axis=1)
        own_row = jnp.sum(jnp.where(chosen, (target - me * rows)[None, :], 0), axis=1)
        count = jnp.minimum(jnp.sum(own.astype(jnp.int32)), SHARE)
        return ours(origins), own_slot, own_row, count[None]

    origins, own_slot, own_row, count = batch(0, BATCH)
    size = BATCH // 2
    where = jnp.stack([me, column]).astype(jnp.int32)
    held = held_by(lax.axis_size("pcol"))
    near, far = ours(named), ours(second_rows)
    segments = [
        [(0, width, 0, 0, width)],
        [(0, b * width, half + b * size, 0, width) for b in range(blocks)],
    ]
    (mine,) = pick([matrix, mate], [after(near, column_one), origins], segments, [(half + blocks * size, width)], work=1)
    segments = [
        [(0, 0, 0, 0, width)] + ([(0, 2 * width, 0, width, cols - 2 * width)] if blocks > 2 else []),
        [(0, 0, 0, cols - width, cols)],
    ]
    (rest,) = pick([matrix, mate], [after(near, mine, hop), far], segments, [(half, 2 * cols - width)], work=6000000000)
    ones = onward(column_one, hop)
    first, *others = axes_order()
    arriving = flip_axes(mine, first)
    mine = mine + arriving
    mine, mates = gather_sum(mine, others)

    wanted = second_rows - me * rows
    wanted = jnp.where((wanted >= 0) & (wanted < rows), wanted, -1)
    keep, give = jnp.where(core == 0, wanted[:half], wanted[half:]), jnp.where(core == 0, wanted[half:], wanted[:half])
    top, given = pick(
        ones, [after(keep, mine), give], [[(0, 0, 0, 0, width)], [(1, 0, 0, 0, width)]], [(half, width)] * 2, (where, held), 6000000000
    )
    block, upper, under, panel = middle_step(
        matrix, after(column_one, top), mine, mates, lower_inv, upper_inv, core[None], own_slot, own_row, count, size
    )
    hops = first_hop(upper), first_hop(under)
    given = swap_cores(given)
    top = after(top, upper) + given
    rest = after(rest, mine)
    arriving = flip_axes(rest, first)
    rest = after(rest, upper) + arriving
    uppers = onward(upper, after(hops[0], rest))
    arriving = flip_axes(top, first)
    top = after(top, hops[0]) + arriving
    unders = onward(under, after(hops[1], top))
    for pair in others:
        arriving = flip_axes(rest, pair)
        rest = after(rest, hops[1]) + arriving
        top = top + flip_axes(top, pair)
    rest_mine, rest_mates = rest, swap_cores(rest)
    top_mine, top_mate = top, swap_cores(top)
    high, low, edge = row_step(where, after(panel, *uppers[1:]), rest_mine, rest_mates, top_mine, top_mate, lower_inv, cols)
    result = finish_step(where, own_row, count, block, ones, uppers, unders, high, low, edge, held)

    crowded = (moved > BATCH) | (jnp.max(shares) > SHARE)
    trips = jnp.where(crowded, (moved + SHARE - 1) // SHARE, 0)

    def more(number, result):
        origins, own_slot, own_row, count = batch(number * SHARE, SHARE)
        rows_here = gather_sum(pick([matrix, mate], [origins], [[(0, 0, 0, 0, cols)]], [(SHARE // 2, cols)])[0])
        raw = jnp.take(jnp.concatenate(rows_here, axis=0), own_slot, axis=0)
        one = product(raw[:, :width], upper_inv[0])
        two = product(raw[:, width : 2 * width] - product(one, panel), upper_inv[1])
        pair = joined(relay(jnp.concatenate([one, two], axis=1)))
        panels = high.astype(F32) + low.astype(F32)
        updated = raw - product(pair, panels)
        updated = jnp.concatenate(
            [jnp.where(first_column, pair, updated[:, : 2 * width]), updated[:, 2 * width :]], axis=1
        )
        return place(result, updated, own_row, count)

    return lax.fori_loop(0, trips, more, result)


def solution(mesh):
    in_specs = (P("prow", "pcol"), P(), P(), P())
    out_specs = P("prow", "pcol")
    return jax.shard_map(shards, mesh=mesh, in_specs=in_specs, out_specs=out_specs, check_vma=False)
```

```python
import jax
import jax.numpy as jnp
from jax import lax
from jax.experimental import pallas as pl
from jax.experimental.pallas import tpu as pltpu
from jax.sharding import PartitionSpec as P

BATCH = 320
SHARE = 80
GROUP = 8
UPPER = 296
F32, BF16 = jnp.float32, jnp.bfloat16
SMEM, VMEM, ANY = (pl.BlockSpec(memory_space=space) for space in (pltpu.SMEM, pltpu.VMEM, pl.ANY))
COSTS = dict(middle=6000000000, rows=10000000000, finish=10000000000, place=1)
PARAMS = pltpu.CompilerParams(vmem_limit_bytes=56 << 20)


def cost(work):
    return pl.CostEstimate(flops=work, bytes_accessed=1, transcendentals=0)


def split(x):
    high = x.astype(BF16)
    return high, (x - high.astype(F32)).astype(BF16)


def mul(left, right):
    dot = lambda a, b: jnp.dot(a, b, preferred_element_type=F32)
    return dot(left[0], right[0]) + (dot(left[0], right[1]) + dot(left[1], right[0]))


def product(left, right):
    return jnp.dot(left, right, precision=lax.Precision.HIGH, preferred_element_type=F32)


def displaced(pivot_row, start_row):
    width = pivot_row.shape[0]
    end_row = start_row + width
    window = start_row + jnp.arange(width, dtype=jnp.int32)
    chosen = jnp.any(pivot_row[None, :] == window[:, None], axis=1)
    unnamed = jnp.logical_not(chosen)
    free_rank = jnp.cumsum(unnamed.astype(jnp.int32)) - 1
    outside = pivot_row >= end_row
    out_rank = jnp.sum(
        (outside[None, :] & (pivot_row[None, :] < pivot_row[:, None])).astype(jnp.int32), axis=1
    )
    matches = unnamed[None, :] & (free_rank[None, :] == out_rank[:, None])
    source = jnp.sum(jnp.where(matches, window[None, :], 0), axis=1)
    return (source, outside)


def pick(sources, lists, pieces, shapes, choice=None, work=1):
    rows, cols = sources[0].shape
    count, many = len(lists), len(sources)
    stacked = 1 if choice else many

    def body(*refs):
        index_refs, source_refs, rest = refs[:count], refs[count : count + many], refs[count + many :]
        if choice:
            where_ref, rest = rest[0], rest[1:]
        out_refs, (chip, sems) = rest[: len(shapes)], rest[len(shapes) :]
        if choice:
            for ref, places in zip(source_refs, choice[1]):

                @pl.when(among(where_ref[1], places))
                def _():
                    copy = pltpu.make_async_copy(ref, chip, sems.at[0])
                    copy.start()
                    copy.wait()
        else:
            copies = [
                pltpu.make_async_copy(ref, chip.at[pl.ds(k * rows, rows)], sems.at[k])
                for k, ref in enumerate(source_refs)
            ]
            for copy in copies:
                copy.start()
            for copy in copies:
                copy.wait()
        for index_ref, vector, segments in zip(index_refs, lists, pieces):

            def step(i, carry):
                start = i * GROUP
                wanted = [index_ref[start + k] for k in range(GROUP)]
                for output, source, row, column, width in segments:
                    values = [chip[pl.ds(jnp.maximum(w, 0), 1), source : source + width] for w in wanted]
                    values = [jnp.where(w >= 0, v, 0.0) for w, v in zip(wanted, values)]
                    for k, value in enumerate(values):
                        out_refs[output][pl.ds(row + start + k, 1), column : column + width] = value
                return carry

            lax.fori_loop(0, vector.shape[0] // GROUP, step, 0)

    return pl.pallas_call(
        body,
        out_shape=[jax.ShapeDtypeStruct(shape, F32) for shape in shapes],
        in_specs=[SMEM] * count + [ANY] * many + ([SMEM] if choice else []),
        out_specs=[VMEM] * len(shapes),
        scratch_shapes=[pltpu.VMEM((stacked * rows, cols), F32), pltpu.SemaphoreType.DMA((stacked,))],
        compiler_params=PARAMS,
        cost_estimate=cost(work),
        name="pick",
    )(*lists, *sources, *([choice[0]] if choice else []))


def among(value, places):
    found = value == places[0]
    for place in places[1:]:
        found = found | (value == place)
    return found


def top_step(ones, wanted, where, held):
    rows, width = ones[0].shape
    half = wanted.shape[0] // 2
    many = len(ones)

    def body(*refs):
        where_ref, wanted_ref, one_refs = refs[0], refs[1], refs[2 : 2 + many]
        keep_ref, give_ref, one, sem = refs[2 + many :]
        for ref, places in zip(one_refs, held):

            @pl.when(among(where_ref[1], places))
            def _():
                copy = pltpu.make_async_copy(ref, one, sem.at[0])
                copy.start()
                copy.wait()

        high, rest = split(one[...])
        low = (one[...] - high.astype(F32) - rest.astype(F32)).astype(BF16)
        for k, ref in enumerate((keep_ref, give_ref)):
            chosen = wanted_ref[k * half : (k + 1) * half, :] == lax.broadcasted_iota(jnp.int32, (half, rows), 1)
            chosen = jnp.where(chosen, 1.0, 0.0).astype(BF16)
            part = lambda x: jnp.dot(chosen, x, preferred_element_type=F32)
            ref[...] = part(high) + (part(rest) + part(low))

    shape = jax.ShapeDtypeStruct((half, width), F32)
    return pl.pallas_call(
        body,
        out_shape=(shape, shape),
        in_specs=[SMEM, VMEM] + [ANY] * many,
        out_specs=(VMEM, VMEM),
        scratch_shapes=[pltpu.VMEM((rows, width), F32), pltpu.SemaphoreType.DMA((1,))],
        compiler_params=PARAMS,
        cost_estimate=cost(6 * 10**9),
        name="top",
    )(where, wanted, *ones)


def split_step(factors):
    def body(factors_ref, high_ref, low_ref):
        for k in range(factors.shape[0]):
            high_ref[k], low_ref[k] = split(factors_ref[k])

    shape = jax.ShapeDtypeStruct(factors.shape, BF16)
    return pl.pallas_call(
        body,
        out_shape=(shape, shape),
        in_specs=[VMEM],
        out_specs=(VMEM, VMEM),
        compiler_params=PARAMS,
        cost_estimate=cost(6000000000),
        name="split",
    )(factors)


def middle_step(matrix, one, mine, mate, lower_high, lower_low, upper, where, slots, targets, count, size):
    rows, cols = matrix.shape
    width = upper.shape[1]
    half = width // 2
    blocks = cols // width
    part = UPPER

    def body(where_ref, slot_ref, target_ref, count_ref, matrix_ref, one_ref, mine_ref, mate_ref, lh_ref, ll_ref, u_ref,
             block_ref, upper_ref, under_ref, panel_ref, raw, pair, new_one):
        block_ref[...] = matrix_ref[...]
        raw[...] = jnp.zeros_like(raw)

        def bring(i, carry):
            slot, row = slot_ref[i], target_ref[i]
            here = slot < size
            at = half + jnp.where(here, slot, slot - size)
            for b in range(blocks):
                value = jnp.where(here, mine_ref[pl.ds(at + b * size, 1), :], mate_ref[pl.ds(at + b * size, 1), :])
                block_ref[pl.ds(row, 1), b * width : (b + 1) * width] = value
                if b == 0:
                    raw[pl.ds(i, 1), :] = value
            return carry

        lax.fori_loop(0, count_ref[0], bring, 0)
        core = where_ref[0] % 2
        first = pl.multiple_of(core * half, half)
        second = pl.multiple_of(half - core * half, half)
        lower = lambda start: (lh_ref[0, :, pl.ds(start, half)], ll_ref[0, :, pl.ds(start, half)])
        panel_ref[...] = mul(lower(first), split(mine_ref[:half, :])) + mul(lower(second), split(mate_ref[:half, :]))

        @pl.when(where_ref[1] == 0)
        def _():
            pair[pl.ds(rows, SHARE), :] = mul(split(raw[...]), split(u_ref[0]))
            new_one[...] = one_ref[...]

            def renew(i, carry):
                new_one[pl.ds(target_ref[i], 1), :] = pair[pl.ds(rows + i, 1), :]
                return carry

            lax.fori_loop(0, count_ref[0], renew, 0)
            rest = block_ref[:, width : 2 * width] - mul(split(new_one[...]), split(panel_ref[...]))
            pair[pl.ds(0, rows), :] = mul(split(rest), split(u_ref[1]))
            upper_ref[...] = pair[:part, :]
            under_ref[...] = pair[part:, :]

    shape = lambda *s: jax.ShapeDtypeStruct(s, F32)
    return pl.pallas_call(
        body,
        out_shape=(shape(rows, cols), shape(part, width), shape(rows + SHARE - part, width), shape(width, width)),
        in_specs=[SMEM] * 4 + [VMEM] * 7,
        out_specs=(VMEM,) * 4,
        scratch_shapes=[pltpu.VMEM(s, F32) for s in ((SHARE, width), (rows + SHARE, width), (rows, width))],
        compiler_params=PARAMS,
        cost_estimate=cost(COSTS["middle"]),
        name="middle",
    )(where, slots, targets, count, matrix, one, mine, mate, lower_high, lower_low, upper)


def row_step(where, panel, mine, mate, top_mine, top_mate, lower_high, lower_low, cols):
    width = panel.shape[0]
    half = width // 2
    blocks = cols // width
    offset = cols - width

    def body(where_ref, panel_ref, mine_ref, mate_ref, tm_ref, tt_ref, lh_ref, ll_ref, high_ref, low_ref, edge_ref, second):
        me, first_column = where_ref[0], where_ref[1] == 0
        core = me % 2
        first = pl.multiple_of(core * half, half)
        other = pl.multiple_of(half - core * half, half)
        lower = lambda k: tuple((lh_ref[k, :, pl.ds(at, half)], ll_ref[k, :, pl.ds(at, half)]) for at in (first, other))
        one, two = lower(0), lower(1)
        tops = (split(tm_ref[...]), split(tt_ref[...]))
        for b in range(blocks):
            at = slice(b * width, (b + 1) * width)
            source = slice((b if b < 1 else b - 1) * width, ((b if b < 1 else b - 1) + 1) * width)
            if b == 1:
                row_one = panel_ref[...]
            else:
                row_one = mul(one[0], split(mine_ref[:, source])) + mul(one[1], split(mate_ref[:, source]))
            kept = jnp.where(first_column, 0.0, row_one) if b < 1 else row_one
            pair = split(kept)
            high_ref[:width, at], low_ref[:width, at] = pair
            rest = slice(offset + b * width, offset + (b + 1) * width)
            second[:half, :] = mine_ref[:, rest] - mul(tops[0], pair)
            second[half:, :] = mate_ref[:, rest] - mul(tops[1], pair)
            row_two = mul(two[0], split(second[:half, :])) + mul(two[1], split(second[half:, :]))
            kept = jnp.where(first_column, 0.0, row_two) if b < 2 else row_two
            high_ref[width:, at], low_ref[width:, at] = split(kept)

            @pl.when(me == 0)
            def _():
                if b >= 1:
                    edge_ref[:, at] = row_one
                else:
                    edge_ref[:half, at] = jnp.where(first_column, mine_ref[:, source], row_one[:half, :])
                    edge_ref[half:, at] = jnp.where(first_column, mate_ref[:, source], row_one[half:, :])

            @pl.when(me != 0)
            def _():
                if b >= 2:
                    edge_ref[:, at] = row_two
                elif b == 1:
                    edge_ref[:half, at] = jnp.where(first_column, second[half:, :], row_two[:half, :])
                    edge_ref[half:, at] = jnp.where(first_column, second[:half, :], row_two[half:, :])
                else:
                    edge_ref[:half, at] = jnp.where(first_column, tt_ref[...], row_two[:half, :])
                    edge_ref[half:, at] = jnp.where(first_column, tm_ref[...], row_two[half:, :])

    return pl.pallas_call(
        body,
        out_shape=(
            jax.ShapeDtypeStruct((2 * width, cols), BF16),
            jax.ShapeDtypeStruct((2 * width, cols), BF16),
            jax.ShapeDtypeStruct((width, cols), F32),
        ),
        in_specs=[SMEM] + [VMEM] * 7,
        out_specs=(VMEM,) * 3,
        scratch_shapes=[pltpu.VMEM((width, width), F32)],
        compiler_params=PARAMS,
        cost_estimate=cost(COSTS["rows"]),
        name="rows",
    )(where, panel, mine, mate, top_mine, top_mate, lower_high, lower_low)


def finish_step(where, targets, count, block, ones, uppers, unders, high, low, edge, held):
    rows, cols = block.shape
    width = ones[0].shape[1]
    part = uppers[0].shape[0]
    parts = len(ones)
    chunk = width // 2

    def body(*refs):
        where_ref, target_ref, count_ref, block_ref, high_ref, low_ref = refs[:6]
        one_refs, upper_refs, under_refs = (refs[6 + parts * k : 6 + parts * (k + 1)] for k in range(3))
        edge_ref, out_ref, one, pair, left_high, left_low, sems = refs[6 + 3 * parts :]
        me, column = where_ref[0], where_ref[1]
        first_column = column == 0
        for k in range(parts):

            @pl.when((me >= 2) & among(column, held[k]))
            def _():
                copies = [
                    pltpu.make_async_copy(one_refs[k], one, sems.at[0]),
                    pltpu.make_async_copy(upper_refs[k], pair.at[pl.ds(0, part)], sems.at[1]),
                    pltpu.make_async_copy(under_refs[k], pair.at[pl.ds(part, rows + SHARE - part)], sems.at[2]),
                ]
                for copy in copies:
                    copy.start()
                for copy in copies:
                    copy.wait()

        @pl.when(me < 2)
        def _():
            copy = pltpu.make_async_copy(edge_ref, out_ref, sems.at[0])
            copy.start()
            copy.wait()

        @pl.when(me >= 2)
        def _():
            def renew(i, carry):
                one[pl.ds(target_ref[i], 1), :] = pair[pl.ds(rows + i, 1), :]
                return carry

            lax.fori_loop(0, count_ref[0], renew, 0)

            for k, source in enumerate((one, pair)):
                at = pl.ds(k * width, width)
                left_high[:, at], left_low[:, at] = split(source[:rows, :])
            for c in range(cols // chunk):
                at = slice(c * chunk, (c + 1) * chunk)
                total = block_ref[:, at] - mul((left_high[...], left_low[...]), (high_ref[:, at], low_ref[:, at]))
                if c * chunk < 2 * width:
                    held_here = (one if c * chunk < width else pair)[:rows, (c * chunk) % width : (c * chunk) % width + chunk]
                    total = jnp.where(first_column, held_here, total)
                out_ref[:, at] = total

    return pl.pallas_call(
        body,
        out_shape=jax.ShapeDtypeStruct((rows, cols), F32),
        in_specs=[SMEM] * 3 + [VMEM] * 3 + [ANY] * (3 * parts + 1),
        out_specs=VMEM,
        scratch_shapes=[
            pltpu.VMEM((rows, width), F32),
            pltpu.VMEM((rows + SHARE, width), F32),
            pltpu.VMEM((rows, 2 * width), BF16),
            pltpu.VMEM((rows, 2 * width), BF16),
            pltpu.SemaphoreType.DMA((3,)),
        ],
        compiler_params=PARAMS,
        cost_estimate=cost(COSTS["finish"]),
        name="finish",
    )(where, targets, count, block, high, low, *ones, *uppers, *unders, edge)


def place(target, rows, where_to, count):
    def body(where_ref, count_ref, target_ref, rows_ref, out_ref):
        out_ref[...] = target_ref[...]

        def step(i, carry):
            out_ref[pl.ds(where_ref[i], 1), :] = rows_ref[pl.ds(i, 1), :]
            return carry

        lax.fori_loop(0, count_ref[0], step, 0)

    return pl.pallas_call(
        body,
        out_shape=jax.ShapeDtypeStruct(target.shape, target.dtype),
        in_specs=[SMEM, SMEM, VMEM, VMEM],
        out_specs=VMEM,
        compiler_params=PARAMS,
        cost_estimate=cost(COSTS["place"]),
        name="place",
    )(where_to, count, target, rows)


def swap_cores(x):
    return lax.ppermute(x, "prow", [(i, i ^ 1) for i in range(lax.axis_size("prow"))])


def axes_order():
    bits = [1 << k for k in range(1, lax.axis_size("prow").bit_length() - 1)]
    return list(zip(bits, bits[len(bits) // 2 :] + bits[: len(bits) // 2]))


def flip_axes(x, pair):
    first, second = pair
    return lax.ppermute(x, "prow", [(i, i ^ (second if i % 2 else first)) for i in range(lax.axis_size("prow"))])


def gather_sum(x, steps=None):
    for pair in axes_order() if steps is None else steps:
        x = x + flip_axes(x, pair)
    return x, swap_cores(x)


def first_hop(x):
    return lax.ppermute(x, "pcol", [(0, 2)])


def onward(x, current):
    count = lax.axis_size("pcol")
    parts = [x]
    for even in range(2, count, 2):
        parts += [current, lax.ppermute(current, "pcol", [(even, even - 1)])]
        if even + 2 < count:
            current = lax.ppermute(current, "pcol", [(even, even + 2)])
        elif even + 1 < count:
            parts.append(lax.ppermute(current, "pcol", [(even, even + 1)]))
    return parts


def relay(x):
    return onward(x, first_hop(x))


def after(x, *others):
    return lax.optimization_barrier((x, *others))[0]


def held_by(count):
    held = [[0]]
    for even in range(2, count, 2):
        held += [[even], [even - 1]]
        if even + 2 >= count and even + 1 < count:
            held.append([even + 1])
    return held


def joined(parts):
    total = parts[1]
    for part in parts[2:]:
        total = total + part
    return jnp.where(lax.axis_index("pcol") == 0, parts[0], total)


def shards(matrix, pivots, lower_inv, upper_inv):
    rows, cols = matrix.shape
    width = lower_inv.shape[1]
    devices = lax.axis_size("prow")
    if rows != width or cols < 2 * width or cols % width or pivots.shape[0] != 2 or devices < 4:
        raise ValueError("unsupported shapes")
    me, column = lax.axis_index("prow"), lax.axis_index("pcol")
    core = me % 2
    first_column = column == 0
    half = width // 2
    blocks = cols // width
    mate = swap_cores(matrix)

    column_one = product(matrix[:, :width], upper_inv[0])
    hop = first_hop(column_one)

    named, taken = pivots[0], pivots[1]
    source_one, outside_one = displaced(named, 0)
    source_two, outside_two = displaced(taken, width)
    same = taken[:, None] == named[None, :]
    again = source_two[:, None] == named[None, :]

    def origin(hit, position):
        return jnp.where(
            jnp.any(hit, axis=1), jnp.sum(jnp.where(hit, source_one[None, :], 0), axis=1), position
        )

    second_rows = origin(same, taken)
    valid = jnp.concatenate(
        [(named >= 2 * width) & jnp.logical_not(jnp.any(same, axis=0)), outside_two]
    )
    target = jnp.concatenate([named, taken])
    origin_row = jnp.concatenate([source_one, origin(again, source_two)])
    rank = jnp.cumsum(valid.astype(jnp.int32)) - 1
    moved = jnp.sum(valid.astype(jnp.int32))
    shares = jnp.sum(
        (valid[None, :] & ((target // rows)[None, :] == jnp.arange(devices, dtype=jnp.int32)[:, None])).astype(
            jnp.int32
        ),
        axis=1,
    )

    def ours(vector):
        size = vector.shape[0] // 2
        wanted = jnp.where(core == 0, vector[:size], vector[size:])
        mine, theirs = wanted - me * rows, wanted - (me + 1 - 2 * core) * rows
        inside = lambda v: (v >= 0) & (v < rows)
        return jnp.where(inside(mine), mine, jnp.where(inside(theirs), rows + theirs, -1))

    def batch(start, size):
        slots = start + jnp.arange(size, dtype=jnp.int32)
        chosen = valid[None, :] & (rank[None, :] == slots[:, None])
        origins = jnp.sum(jnp.where(chosen, origin_row[None, :], 0), axis=1)
        own = valid & (rank >= start) & (rank < start + size) & (target // rows == me)
        own_rank = jnp.cumsum(own.astype(jnp.int32)) - 1
        chosen = own[None, :] & (own_rank[None, :] == jnp.arange(SHARE, dtype=jnp.int32)[:, None])
        slot = (rank - start + core * (size // 2)) % size
        own_slot = jnp.sum(jnp.where(chosen, slot[None, :], 0), axis=1)
        own_row = jnp.sum(jnp.where(chosen, (target - me * rows)[None, :], 0), axis=1)
        count = jnp.minimum(jnp.sum(own.astype(jnp.int32)), SHARE)
        return ours(origins), own_slot, own_row, count[None]

    origins, own_slot, own_row, count = batch(0, BATCH)
    size = BATCH // 2
    where = jnp.stack([me, column]).astype(jnp.int32)
    held = held_by(lax.axis_size("pcol"))
    near, far = ours(named), ours(second_rows)
    segments = [
        [(0, width, 0, 0, width)],
        [(0, b * width, half + b * size, 0, width) for b in range(blocks)],
    ]
    (mine,) = pick([matrix, mate], [after(near, column_one), origins], segments, [(half + blocks * size, width)], work=1)
    segments = [
        [(0, 0, 0, 0, width)] + ([(0, 2 * width, 0, width, cols - 2 * width)] if blocks > 2 else []),
        [(0, 0, 0, cols - width, cols)],
    ]
    (rest,) = pick([matrix, mate], [after(near, mine), far], segments, [(half, 2 * cols - width)], work=6000000000)
    ones = onward(column_one, hop)
    first, *others = axes_order()
    arriving = flip_axes(mine, first)
    lowers = split_step(after(lower_inv, hop))
    mine = after(mine, lowers[0]) + arriving
    mine, mates = gather_sum(mine, others)

    wanted = second_rows - me * rows
    keep, give = jnp.where(core == 0, wanted[:half], wanted[half:]), jnp.where(core == 0, wanted[half:], wanted[:half])
    top, given = top_step(ones, jnp.concatenate([after(keep, mine), give])[:, None], where, held)
    block, upper, under, panel = middle_step(
        matrix, after(column_one, top), mine, mates, *lowers, upper_inv, where, own_slot, own_row, count, size
    )
    hops = first_hop(upper), first_hop(under)
    given = swap_cores(given)
    top = after(top, upper) + given
    rest = after(rest, mine)
    arriving = flip_axes(rest, first)
    rest = after(rest, upper) + arriving
    uppers = onward(upper, hops[0])
    unders = onward(under, hops[1])
    arriving = flip_axes(top, first)
    top = after(top, upper, hops[1]) + arriving
    for pair in others:
        arriving = flip_axes(rest, pair)
        over = flip_axes(top, pair)
        rest = after(rest, upper, hops[0]) + arriving
        top = after(top, upper) + over
    rest_mine, rest_mates = rest, swap_cores(rest)
    top_mine, top_mate = top, swap_cores(top)
    high, low, edge = row_step(where, after(panel, *uppers[1:]), rest_mine, rest_mates, top_mine, top_mate, *lowers, cols)
    result = finish_step(where, own_row, count, block, ones, uppers, unders, high, low, edge, held)

    crowded = (moved > BATCH) | (jnp.max(shares) > SHARE)
    trips = jnp.where(crowded, (moved + SHARE - 1) // SHARE, 0)

    def more(number, result):
        origins, own_slot, own_row, count = batch(number * SHARE, SHARE)
        rows_here = gather_sum(pick([matrix, mate], [origins], [[(0, 0, 0, 0, cols)]], [(SHARE // 2, cols)])[0])
        raw = jnp.take(jnp.concatenate(rows_here, axis=0), own_slot, axis=0)
        one = product(raw[:, :width], upper_inv[0])
        two = product(raw[:, width : 2 * width] - product(one, panel), upper_inv[1])
        pair = joined(relay(jnp.concatenate([one, two], axis=1)))
        panels = high.astype(F32) + low.astype(F32)
        updated = raw - product(pair, panels)
        updated = jnp.concatenate(
            [jnp.where(first_column, pair, updated[:, : 2 * width]), updated[:, 2 * width :]], axis=1
        )
        return place(result, updated, own_row, count)

    return lax.fori_loop(0, trips, more, result)


def solution(mesh):
    in_specs = (P("prow", "pcol"), P(), P(), P())
    out_specs = P("prow", "pcol")
    return jax.shard_map(shards, mesh=mesh, in_specs=in_specs, out_specs=out_specs, check_vma=False)
```

```python
import jax
import jax.numpy as jnp
from jax import lax
from jax.experimental import pallas as pl
from jax.experimental.pallas import tpu as pltpu
from jax.sharding import PartitionSpec as P

BATCH = 304
SHARE = 72
SMALL = 64
GROUP = 8
UPPER = 296
F32, BF16 = jnp.float32, jnp.bfloat16
SMEM, VMEM, ANY = (pl.BlockSpec(memory_space=space) for space in (pltpu.SMEM, pltpu.VMEM, pl.ANY))
COSTS = dict(middle=6000000000, rows=10000000000, finish=10000000000, place=1)
PARAMS = pltpu.CompilerParams(vmem_limit_bytes=56 << 20)


def cost(work):
    return pl.CostEstimate(flops=work, bytes_accessed=1, transcendentals=0)


def split(x):
    high = x.astype(BF16)
    return high, (x - high.astype(F32)).astype(BF16)


def mul(left, right):
    dot = lambda a, b: jnp.dot(a, b, preferred_element_type=F32)
    return dot(left[0], right[0]) + (dot(left[0], right[1]) + dot(left[1], right[0]))


def product(left, right):
    return jnp.dot(left, right, precision=lax.Precision.HIGH, preferred_element_type=F32)


def displaced(pivot_row, start_row):
    width = pivot_row.shape[0]
    end_row = start_row + width
    window = start_row + jnp.arange(width, dtype=jnp.int32)
    chosen = jnp.any(pivot_row[None, :] == window[:, None], axis=1)
    unnamed = jnp.logical_not(chosen)
    free_rank = jnp.cumsum(unnamed.astype(jnp.int32)) - 1
    outside = pivot_row >= end_row
    out_rank = jnp.sum(
        (outside[None, :] & (pivot_row[None, :] < pivot_row[:, None])).astype(jnp.int32), axis=1
    )
    matches = unnamed[None, :] & (free_rank[None, :] == out_rank[:, None])
    source = jnp.sum(jnp.where(matches, window[None, :], 0), axis=1)
    return (source, outside)


def pick(sources, lists, pieces, shapes, choice=None, work=1):
    rows, cols = sources[0].shape
    count, many = len(lists), len(sources)
    stacked = 1 if choice else many

    def body(*refs):
        index_refs, source_refs, rest = refs[:count], refs[count : count + many], refs[count + many :]
        if choice:
            where_ref, rest = rest[0], rest[1:]
        out_refs, (chip, sems) = rest[: len(shapes)], rest[len(shapes) :]
        if choice:
            for ref, places in zip(source_refs, choice[1]):

                @pl.when(among(where_ref[1], places))
                def _():
                    copy = pltpu.make_async_copy(ref, chip, sems.at[0])
                    copy.start()
                    copy.wait()
        else:
            copies = [
                pltpu.make_async_copy(ref, chip.at[pl.ds(k * rows, rows)], sems.at[k])
                for k, ref in enumerate(source_refs)
            ]
            for copy in copies:
                copy.start()
            for copy in copies:
                copy.wait()
        for index_ref, vector, segments in zip(index_refs, lists, pieces):

            def step(i, carry):
                start = i * GROUP
                wanted = [index_ref[start + k] for k in range(GROUP)]
                for output, source, row, column, width in segments:
                    values = [chip[pl.ds(jnp.maximum(w, 0), 1), source : source + width] for w in wanted]
                    values = [jnp.where(w >= 0, v, 0.0) for w, v in zip(wanted, values)]
                    for k, value in enumerate(values):
                        out_refs[output][pl.ds(row + start + k, 1), column : column + width] = value
                return carry

            lax.fori_loop(0, vector.shape[0] // GROUP, step, 0)

    return pl.pallas_call(
        body,
        out_shape=[jax.ShapeDtypeStruct(shape, F32) for shape in shapes],
        in_specs=[SMEM] * count + [ANY] * many + ([SMEM] if choice else []),
        out_specs=[VMEM] * len(shapes),
        scratch_shapes=[pltpu.VMEM((stacked * rows, cols), F32), pltpu.SemaphoreType.DMA((stacked,))],
        compiler_params=PARAMS,
        cost_estimate=cost(work),
        name="pick",
    )(*lists, *sources, *([choice[0]] if choice else []))


def among(value, places):
    found = value == places[0]
    for place in places[1:]:
        found = found | (value == place)
    return found


def top_step(ones, wanted, where, held):
    rows, width = ones[0].shape
    half = wanted.shape[0] // 2
    many = len(ones)

    def body(*refs):
        where_ref, wanted_ref, one_refs = refs[0], refs[1], refs[2 : 2 + many]
        keep_ref, give_ref, one, sem = refs[2 + many :]
        for ref, places in zip(one_refs, held):

            @pl.when(among(where_ref[1], places))
            def _():
                copy = pltpu.make_async_copy(ref, one, sem.at[0])
                copy.start()
                copy.wait()

        high, rest = split(one[...])
        low = (one[...] - high.astype(F32) - rest.astype(F32)).astype(BF16)
        for k, ref in enumerate((keep_ref, give_ref)):
            chosen = wanted_ref[k * half : (k + 1) * half, :] == lax.broadcasted_iota(jnp.int32, (half, rows), 1)
            chosen = jnp.where(chosen, 1.0, 0.0).astype(BF16)
            part = lambda x: jnp.dot(chosen, x, preferred_element_type=F32)
            ref[...] = part(high) + (part(rest) + part(low))

    shape = jax.ShapeDtypeStruct((half, width), F32)
    return pl.pallas_call(
        body,
        out_shape=(shape, shape),
        in_specs=[SMEM, VMEM] + [ANY] * many,
        out_specs=(VMEM, VMEM),
        scratch_shapes=[pltpu.VMEM((rows, width), F32), pltpu.SemaphoreType.DMA((1,))],
        compiler_params=PARAMS,
        cost_estimate=cost(6 * 10**9),
        name="top",
    )(where, wanted, *ones)


def split_step(factors):
    def body(factors_ref, high_ref, low_ref):
        for k in range(factors.shape[0]):
            high_ref[k], low_ref[k] = split(factors_ref[k])

    shape = jax.ShapeDtypeStruct(factors.shape, BF16)
    return pl.pallas_call(
        body,
        out_shape=(shape, shape),
        in_specs=[VMEM],
        out_specs=(VMEM, VMEM),
        compiler_params=PARAMS,
        cost_estimate=cost(6000000000),
        name="split",
    )(factors)


def middle_step(matrix, one, mine, mate, lower_high, lower_low, upper, where, slots, targets, count, size):
    rows, cols = matrix.shape
    width = upper.shape[1]
    half = width // 2
    blocks = cols // width
    part = UPPER

    def body(where_ref, slot_ref, target_ref, count_ref, matrix_ref, one_ref, mine_ref, mate_ref, lh_ref, ll_ref, u_ref,
             block_ref, upper_ref, under_ref, panel_ref, raw, pair, new_one):
        block_ref[...] = matrix_ref[...]
        raw[...] = jnp.zeros_like(raw)

        def bring(i, carry):
            slot, row = slot_ref[i], target_ref[i]
            here = slot < size
            at = half + jnp.where(here, slot, slot - size)
            for b in range(blocks):
                value = jnp.where(here, mine_ref[pl.ds(at + b * size, 1), :], mate_ref[pl.ds(at + b * size, 1), :])
                block_ref[pl.ds(row, 1), b * width : (b + 1) * width] = value
                if b == 0:
                    raw[pl.ds(i, 1), :] = value
            return carry

        lax.fori_loop(0, count_ref[0], bring, 0)
        core = where_ref[0] % 2
        first = pl.multiple_of(core * half, half)
        second = pl.multiple_of(half - core * half, half)
        lower = lambda start: (lh_ref[0, :, pl.ds(start, half)], ll_ref[0, :, pl.ds(start, half)])
        panel_ref[...] = mul(lower(first), split(mine_ref[:half, :])) + mul(lower(second), split(mate_ref[:half, :]))

        @pl.when(where_ref[1] == 0)
        def _():
            pair[pl.ds(rows, SHARE), :] = mul(split(raw[...]), split(u_ref[0]))
            new_one[...] = one_ref[...]

            def renew(i, carry):
                new_one[pl.ds(target_ref[i], 1), :] = pair[pl.ds(rows + i, 1), :]
                return carry

            lax.fori_loop(0, count_ref[0], renew, 0)
            rest = block_ref[:, width : 2 * width] - mul(split(new_one[...]), split(panel_ref[...]))
            pair[pl.ds(0, rows), :] = mul(split(rest), split(u_ref[1]))
            upper_ref[...] = pair[:part, :]
            under_ref[...] = pair[part:, :]

    shape = lambda *s: jax.ShapeDtypeStruct(s, F32)
    return pl.pallas_call(
        body,
        out_shape=(shape(rows, cols), shape(part, width), shape(rows + SHARE - part, width), shape(width, width)),
        in_specs=[SMEM] * 4 + [VMEM] * 7,
        out_specs=(VMEM,) * 4,
        scratch_shapes=[pltpu.VMEM(s, F32) for s in ((SHARE, width), (rows + SHARE, width), (rows, width))],
        compiler_params=PARAMS,
        cost_estimate=cost(COSTS["middle"]),
        name="middle",
    )(where, slots, targets, count, matrix, one, mine, mate, lower_high, lower_low, upper)


def row_step(where, panel, mine, mate, top_mine, top_mate, lower_high, lower_low, cols):
    width = panel.shape[0]
    half = width // 2
    blocks = cols // width
    offset = cols - width

    def body(where_ref, panel_ref, mine_ref, mate_ref, tm_ref, tt_ref, lh_ref, ll_ref, high_ref, low_ref, edge_ref, second):
        me, first_column = where_ref[0], where_ref[1] == 0
        core = me % 2
        first = pl.multiple_of(core * half, half)
        other = pl.multiple_of(half - core * half, half)
        lower = lambda k: tuple((lh_ref[k, :, pl.ds(at, half)], ll_ref[k, :, pl.ds(at, half)]) for at in (first, other))
        one, two = lower(0), lower(1)
        tops = (split(tm_ref[...]), split(tt_ref[...]))
        for b in range(blocks):
            at = slice(b * width, (b + 1) * width)
            source = slice((b if b < 1 else b - 1) * width, ((b if b < 1 else b - 1) + 1) * width)
            if b == 1:
                row_one = panel_ref[...]
            else:
                row_one = mul(one[0], split(mine_ref[:, source])) + mul(one[1], split(mate_ref[:, source]))
            kept = jnp.where(first_column, 0.0, row_one) if b < 1 else row_one
            pair = split(kept)
            high_ref[:width, at], low_ref[:width, at] = pair
            rest = slice(offset + b * width, offset + (b + 1) * width)
            second[:half, :] = mine_ref[:, rest] - mul(tops[0], pair)
            second[half:, :] = mate_ref[:, rest] - mul(tops[1], pair)
            row_two = mul(two[0], split(second[:half, :])) + mul(two[1], split(second[half:, :]))
            kept = jnp.where(first_column, 0.0, row_two) if b < 2 else row_two
            high_ref[width:, at], low_ref[width:, at] = split(kept)

            @pl.when(me == 0)
            def _():
                if b >= 1:
                    edge_ref[:, at] = row_one
                else:
                    edge_ref[:half, at] = jnp.where(first_column, mine_ref[:, source], row_one[:half, :])
                    edge_ref[half:, at] = jnp.where(first_column, mate_ref[:, source], row_one[half:, :])

            @pl.when(me != 0)
            def _():
                if b >= 2:
                    edge_ref[:, at] = row_two
                elif b == 1:
                    edge_ref[:half, at] = jnp.where(first_column, second[half:, :], row_two[:half, :])
                    edge_ref[half:, at] = jnp.where(first_column, second[:half, :], row_two[half:, :])
                else:
                    edge_ref[:half, at] = jnp.where(first_column, tt_ref[...], row_two[:half, :])
                    edge_ref[half:, at] = jnp.where(first_column, tm_ref[...], row_two[half:, :])

    return pl.pallas_call(
        body,
        out_shape=(
            jax.ShapeDtypeStruct((2 * width, cols), BF16),
            jax.ShapeDtypeStruct((2 * width, cols), BF16),
            jax.ShapeDtypeStruct((width, cols), F32),
        ),
        in_specs=[SMEM] + [VMEM] * 7,
        out_specs=(VMEM,) * 3,
        scratch_shapes=[pltpu.VMEM((width, width), F32)],
        compiler_params=PARAMS,
        cost_estimate=cost(COSTS["rows"]),
        name="rows",
    )(where, panel, mine, mate, top_mine, top_mate, lower_high, lower_low)


def finish_step(where, targets, count, block, ones, uppers, unders, high, low, edge, held):
    rows, cols = block.shape
    width = ones[0].shape[1]
    part = uppers[0].shape[0]
    parts = len(ones)
    chunk = width // 2

    def body(*refs):
        where_ref, target_ref, count_ref, block_ref, high_ref, low_ref = refs[:6]
        one_refs, upper_refs, under_refs = (refs[6 + parts * k : 6 + parts * (k + 1)] for k in range(3))
        edge_ref, out_ref, one, pair, left_high, left_low, sems = refs[6 + 3 * parts :]
        me, column = where_ref[0], where_ref[1]
        first_column = column == 0
        for k in range(parts):

            @pl.when((me >= 2) & among(column, held[k]))
            def _():
                copies = [
                    pltpu.make_async_copy(one_refs[k], one, sems.at[0]),
                    pltpu.make_async_copy(upper_refs[k], pair.at[pl.ds(0, part)], sems.at[1]),
                    pltpu.make_async_copy(under_refs[k], pair.at[pl.ds(part, rows + SHARE - part)], sems.at[2]),
                ]
                for copy in copies:
                    copy.start()
                for copy in copies:
                    copy.wait()

        @pl.when(me < 2)
        def _():
            copy = pltpu.make_async_copy(edge_ref, out_ref, sems.at[0])
            copy.start()
            copy.wait()

        @pl.when(me >= 2)
        def _():
            def renew(i, carry):
                one[pl.ds(target_ref[i], 1), :] = pair[pl.ds(rows + i, 1), :]
                return carry

            lax.fori_loop(0, count_ref[0], renew, 0)

            for k, source in enumerate((one, pair)):
                at = pl.ds(k * width, width)
                left_high[:, at], left_low[:, at] = split(source[:rows, :])
            for c in range(cols // chunk):
                at = slice(c * chunk, (c + 1) * chunk)
                total = block_ref[:, at] - mul((left_high[...], left_low[...]), (high_ref[:, at], low_ref[:, at]))
                if c * chunk < 2 * width:
                    held_here = (one if c * chunk < width else pair)[:rows, (c * chunk) % width : (c * chunk) % width + chunk]
                    total = jnp.where(first_column, held_here, total)
                out_ref[:, at] = total

    return pl.pallas_call(
        body,
        out_shape=jax.ShapeDtypeStruct((rows, cols), F32),
        in_specs=[SMEM] * 3 + [VMEM] * 3 + [ANY] * (3 * parts + 1),
        out_specs=VMEM,
        scratch_shapes=[
            pltpu.VMEM((rows, width), F32),
            pltpu.VMEM((rows + SHARE, width), F32),
            pltpu.VMEM((rows, 2 * width), BF16),
            pltpu.VMEM((rows, 2 * width), BF16),
            pltpu.SemaphoreType.DMA((3,)),
        ],
        compiler_params=PARAMS,
        cost_estimate=cost(COSTS["finish"]),
        name="finish",
    )(where, targets, count, block, high, low, *ones, *uppers, *unders, edge)


def place(target, rows, where_to, count):
    def body(where_ref, count_ref, target_ref, rows_ref, out_ref):
        out_ref[...] = target_ref[...]

        def step(i, carry):
            out_ref[pl.ds(where_ref[i], 1), :] = rows_ref[pl.ds(i, 1), :]
            return carry

        lax.fori_loop(0, count_ref[0], step, 0)

    return pl.pallas_call(
        body,
        out_shape=jax.ShapeDtypeStruct(target.shape, target.dtype),
        in_specs=[SMEM, SMEM, VMEM, VMEM],
        out_specs=VMEM,
        compiler_params=PARAMS,
        cost_estimate=cost(COSTS["place"]),
        name="place",
    )(where_to, count, target, rows)


def swap_cores(x):
    return lax.ppermute(x, "prow", [(i, i ^ 1) for i in range(lax.axis_size("prow"))])


def axes_order():
    bits = [1 << k for k in range(1, lax.axis_size("prow").bit_length() - 1)]
    return list(zip(bits, bits[len(bits) // 2 :] + bits[: len(bits) // 2]))


def flip_axes(x, pair):
    first, second = pair
    return lax.ppermute(x, "prow", [(i, i ^ (second if i % 2 else first)) for i in range(lax.axis_size("prow"))])


def gather_sum(x, steps=None):
    for pair in axes_order() if steps is None else steps:
        x = x + flip_axes(x, pair)
    return x, swap_cores(x)


def first_hop(x):
    return lax.ppermute(x, "pcol", [(0, 2)])


def onward(x, current):
    count = lax.axis_size("pcol")
    parts = [x]
    for even in range(2, count, 2):
        parts += [current, lax.ppermute(current, "pcol", [(even, even - 1)])]
        if even + 2 < count:
            current = lax.ppermute(current, "pcol", [(even, even + 2)])
        elif even + 1 < count:
            parts.append(lax.ppermute(current, "pcol", [(even, even + 1)]))
    return parts


def relay(x):
    return onward(x, first_hop(x))


def after(x, *others):
    return lax.optimization_barrier((x, *others))[0]


def held_by(count):
    held = [[0]]
    for even in range(2, count, 2):
        held += [[even], [even - 1]]
        if even + 2 >= count and even + 1 < count:
            held.append([even + 1])
    return held


def joined(parts):
    total = parts[1]
    for part in parts[2:]:
        total = total + part
    return jnp.where(lax.axis_index("pcol") == 0, parts[0], total)


def shards(matrix, pivots, lower_inv, upper_inv):
    rows, cols = matrix.shape
    width = lower_inv.shape[1]
    devices = lax.axis_size("prow")
    if rows != width or cols < 2 * width or cols % width or pivots.shape[0] != 2 or devices < 4:
        raise ValueError("unsupported shapes")
    me, column = lax.axis_index("prow"), lax.axis_index("pcol")
    core = me % 2
    first_column = column == 0
    half = width // 2
    blocks = cols // width
    mate = swap_cores(matrix)

    column_one = product(matrix[:, :width], upper_inv[0])
    hop = first_hop(column_one)

    named, taken = pivots[0], pivots[1]
    source_one, outside_one = displaced(named, 0)
    source_two, outside_two = displaced(taken, width)
    same = taken[:, None] == named[None, :]
    again = source_two[:, None] == named[None, :]

    def origin(hit, position):
        return jnp.where(
            jnp.any(hit, axis=1), jnp.sum(jnp.where(hit, source_one[None, :], 0), axis=1), position
        )

    second_rows = origin(same, taken)
    valid = jnp.concatenate(
        [(named >= 2 * width) & jnp.logical_not(jnp.any(same, axis=0)), outside_two]
    )
    target = jnp.concatenate([named, taken])
    origin_row = jnp.concatenate([source_one, origin(again, source_two)])
    rank = jnp.cumsum(valid.astype(jnp.int32)) - 1
    moved = jnp.sum(valid.astype(jnp.int32))
    shares = jnp.sum(
        (valid[None, :] & ((target // rows)[None, :] == jnp.arange(devices, dtype=jnp.int32)[:, None])).astype(
            jnp.int32
        ),
        axis=1,
    )

    def ours(vector):
        size = vector.shape[0] // 2
        wanted = jnp.where(core == 0, vector[:size], vector[size:])
        mine, theirs = wanted - me * rows, wanted - (me + 1 - 2 * core) * rows
        inside = lambda v: (v >= 0) & (v < rows)
        return jnp.where(inside(mine), mine, jnp.where(inside(theirs), rows + theirs, -1))

    def batch(start, size):
        slots = start + jnp.arange(size, dtype=jnp.int32)
        chosen = valid[None, :] & (rank[None, :] == slots[:, None])
        origins = jnp.sum(jnp.where(chosen, origin_row[None, :], 0), axis=1)
        own = valid & (rank >= start) & (rank < start + size) & (target // rows == me)
        own_rank = jnp.cumsum(own.astype(jnp.int32)) - 1
        chosen = own[None, :] & (own_rank[None, :] == jnp.arange(SHARE, dtype=jnp.int32)[:, None])
        slot = (rank - start + core * (size // 2)) % size
        own_slot = jnp.sum(jnp.where(chosen, slot[None, :], 0), axis=1)
        own_row = jnp.sum(jnp.where(chosen, (target - me * rows)[None, :], 0), axis=1)
        count = jnp.minimum(jnp.sum(own.astype(jnp.int32)), SHARE)
        return ours(origins), own_slot, own_row, count[None]

    origins, own_slot, own_row, count = batch(0, BATCH)
    size = BATCH // 2
    where = jnp.stack([me, column]).astype(jnp.int32)
    held = held_by(lax.axis_size("pcol"))
    near, far = ours(named), ours(second_rows)
    segments = [
        [(0, width, 0, 0, width)],
        [(0, b * width, half + b * size, 0, width) for b in range(blocks)],
    ]
    (mine,) = pick([matrix, mate], [after(near, column_one), origins], segments, [(half + blocks * size, width)], work=1)
    segments = [
        [(0, 0, 0, 0, width)] + ([(0, 2 * width, 0, width, cols - 2 * width)] if blocks > 2 else []),
        [(0, 0, 0, cols - width, cols)],
    ]
    (rest,) = pick([matrix, mate], [after(near, mine), far], segments, [(half, 2 * cols - width)], work=6000000000)
    ones = onward(column_one, hop)
    first, *others = axes_order()
    arriving = flip_axes(mine, first)
    lowers = split_step(after(lower_inv, hop))
    mine = after(mine, lowers[0]) + arriving
    mine, mates = gather_sum(mine, others)

    wanted = second_rows - me * rows
    keep, give = jnp.where(core == 0, wanted[:half], wanted[half:]), jnp.where(core == 0, wanted[half:], wanted[:half])
    top, given = top_step(ones, jnp.concatenate([after(keep, mine), give])[:, None], where, held)
    block, upper, under, panel = middle_step(
        matrix, column_one, mine, mates, *lowers, upper_inv, where, own_slot, own_row, count, size
    )
    hops = first_hop(upper), first_hop(under)
    given = swap_cores(given)
    top = after(top, upper) + given
    rest = after(rest, mine)
    arriving = flip_axes(rest, first)
    rest = after(rest, upper) + arriving
    uppers = onward(upper, hops[0])
    unders = onward(under, hops[1])
    arriving = flip_axes(top, first)
    top = after(top, upper, hops[1]) + arriving
    for pair in others:
        arriving = flip_axes(rest, pair)
        over = flip_axes(top, pair)
        rest = after(rest, upper, hops[0]) + arriving
        top = after(top, upper) + over
    rest_mine, rest_mates = rest, swap_cores(rest)
    top_mine, top_mate = top, swap_cores(top)
    high, low, edge = row_step(where, after(panel, *uppers[1:]), rest_mine, rest_mates, top_mine, top_mate, *lowers, cols)
    result = finish_step(where, own_row, count, block, ones, uppers, unders, high, low, edge, held)

    crowded = (moved > BATCH) | (jnp.max(shares) > SHARE)
    trips = jnp.where(crowded, (moved + SMALL - 1) // SMALL, 0)

    def more(number, result):
        origins, own_slot, own_row, count = batch(number * SMALL, SMALL)
        rows_here = gather_sum(pick([matrix, mate], [origins], [[(0, 0, 0, 0, cols)]], [(SMALL // 2, cols)])[0])
        raw = jnp.take(jnp.concatenate(rows_here, axis=0), own_slot, axis=0)
        one = product(raw[:, :width], upper_inv[0])
        two = product(raw[:, width : 2 * width] - product(one, panel), upper_inv[1])
        pair = joined(relay(jnp.concatenate([one, two], axis=1)))
        panels = high.astype(F32) + low.astype(F32)
        updated = raw - product(pair, panels)
        updated = jnp.concatenate(
            [jnp.where(first_column, pair, updated[:, : 2 * width]), updated[:, 2 * width :]], axis=1
        )
        return place(result, updated, own_row, count)

    return lax.fori_loop(0, trips, more, result)


def solution(mesh):
    in_specs = (P("prow", "pcol"), P(), P(), P())
    out_specs = P("prow", "pcol")
    return jax.shard_map(shards, mesh=mesh, in_specs=in_specs, out_specs=out_specs, check_vma=False)
```
